32 devices in a mesh: tm: 8 (over z, x), user: 4 (over y, core).
Axes of the slice: x: 2, y: 2, z: 4, core: 2. Of those that a mesh axis runs over, the one named last changes fastest.
Arguments:
- user_factor: bfloat16 [8192, 128], P('user'), may hold values from -2.390625 to 2.390625
- user_tangent: bfloat16 [8192, 128], P('user'), may hold values from -2.390625 to 2.390625
- item_factor: bfloat16 [512, 128], P('tm'), may hold values from -2.390625 to 2.390625
- item_tangent: bfloat16 [512, 128], P('tm'), may hold values from -2.390625 to 2.390625
- time_factor: bfloat16 [128, 128], P('tm'), may hold values from -2.390625 to 2.390625
- time_tangent: bfloat16 [128, 128], P('tm'), may hold values from -2.390625 to 2.390625
- send_list: int32 [8, 4, 4, 4], P('tm', 'user'), may hold values from 0 to 15
- tile_slot: int32 [8, 4, 16], P('tm', 'user'), may hold values from 0 to 15, as said below
- tile_item: int32 [8, 4, 16], P('tm', 'user'), may hold values from 0 to 1
- tile_count: int32 [8, 4], P('tm', 'user'), may hold values from 8 to 16, as said below
Outputs:
- user_hvp: float32 [8192, 128], P('user')
- item_hvp: float32 [512, 128], P('tm')
- time_hvp: float32 [128, 128], P('tm')
The draws below stay inside these ranges and needn't reach their ends.
Inputs may be any that keep to these rules, and one draw needn't show every extreme that they name: `tile_slot`: for each (a, j) the first min(16, 16) entries are distinct. `tile_count`: some pair (a, j) has exactly 16 tiles in every draw.
All inputs are finite; a program needn't handle non-finite values.
Results may differ from the reference program's by a relative error of at most 0.0013.
Values may be sent and summed in bfloat16 or wider, within the bound.
No kernel may reach another device: no remote copies, remote signals or barrier semaphores. Data moves between devices by JAX's collectives and lax.ppermute only.
A program may use at most 64 MiB of HBM per device.

```python
import math
import jax
import jax.numpy as jnp
import numpy as np
from jax import lax

R = 128
UB = 128
IT = 256
TS = 16
NB_DEV = 16
SLOTS = 4
NT_CAP = 16
USERS = 8192
ITEMS = 512
ITEM_TILES = 2
STEPS = 128
N_TM = 8
N_USER = 4


def draw_tile_count(key, part):
    first_key, second_key, third_key = jax.random.split(key, 3)
    pairs = N_TM * N_USER
    low = NT_CAP // 2
    base = low + jax.random.randint(first_key, (pairs,), 0, NT_CAP - low + 1)
    position = jax.random.randint(second_key, (), 0, pairs)
    other = (position + 1 + jax.random.randint(third_key, (), 0, pairs - 1)) % pairs
    numbers = jnp.arange(pairs)
    filled = jnp.where(numbers == other, low, base)
    filled = jnp.where(numbers == position, NT_CAP, filled)
    return filled.reshape(N_TM, N_USER).astype(jnp.int32)


def draw_tile_slot(key, part):
    first_key, second_key = jax.random.split(jax.random.fold_in(key, 7))
    pairs = N_TM * N_USER
    width = N_USER * SLOTS
    scores = jax.random.randint(first_key, (pairs, width), 0, 1 << 20) * width + jnp.arange(width, dtype=jnp.int32)[None, :]
    order = jnp.argsort(scores, axis=1).astype(jnp.int32)
    extra = jax.random.randint(second_key, (pairs, NT_CAP), 0, width).astype(jnp.int32)
    joined = jnp.concatenate([order, extra], axis=1)[:, :NT_CAP]
    return joined.reshape(N_TM, N_USER, NT_CAP).astype(jnp.int32)


def plant(array, key, low, high):
    index_at = [jax.random.randint(jax.random.fold_in(key, axis), (), 0, length) for axis, length in enumerate(array.shape)]
    longest = array.shape.index(max(array.shape))
    neighbour = index_at[:longest] + [(index_at[longest] + 1) % array.shape[longest]] + index_at[longest + 1:]
    return array.at[tuple(index_at)].set(low).at[tuple(neighbour)].set(high)


def level_of(key, shape, cuts, least, top_value):
    def one(dim, blocks):
        heights = jax.random.uniform(jax.random.fold_in(jax.random.fold_in(key, 6), dim), (blocks,), jnp.float32, least / len(cuts), top_value / len(cuts))
        return jnp.repeat(jnp.exp(heights), shape[dim] // blocks).reshape((-1,) + (1,) * (len(shape) - dim - 1))

    factor_of = one(*cuts[0])
    for cut in cuts[1:]:
        factor_of = factor_of * one(*cut)
    return factor_of


def rank_table(number_of, slope):
    portions = [(1 << 20) // math.isqrt(grade ** slope) + 1 for grade in range(1, number_of + 1)]
    scale = 1 + sum(portions) // (1 << 30)
    return np.cumsum(np.array([max(1, weight // scale) for weight in portions]))


def ranked_ids(rng, shape, count, skew):
    grid = rank_table(count, skew)
    ticket = jax.random.randint(jax.random.fold_in(rng, 1), shape, 0, int(grid[count - 1]))
    grade = jnp.searchsorted(jnp.asarray(grid, jnp.int32), ticket, side="right")
    return jax.random.permutation(jax.random.fold_in(rng, 2), count)[grade].astype(jnp.int32)


def bell_draw(stream_key, shape, scale, most, pieces=(), kind=jnp.bfloat16):
    array = jax.random.normal(stream_key, shape, jnp.float32) * scale
    if len(pieces) > 0:
        array = level_of(stream_key, shape, pieces, -0.22, 0.18) * array
    return jnp.clip(array, min=-most, max=most).astype(kind)


def setup_inputs(seed: int = 0) -> dict:
    arg_keys = jax.random.split(jax.random.key(seed), 11)
    user_factor = bell_draw(arg_keys[0], (USERS, R), 0.4, 2.390625, ((0, 4),))
    user_tangent = bell_draw(arg_keys[1], (USERS, R), 0.4, 2.390625, ((0, 4),))
    item_factor = bell_draw(arg_keys[2], (ITEMS, R), 0.4, 2.390625, ((0, 8),))
    item_tangent = bell_draw(arg_keys[3], (ITEMS, R), 0.4, 2.390625, ((0, 8),))
    time_factor = bell_draw(arg_keys[4], (STEPS, R), 0.4, 2.390625, ((0, 8),))
    time_tangent = bell_draw(arg_keys[5], (STEPS, R), 0.4, 2.390625, ((0, 8),))
    send_list = plant(jax.random.randint(arg_keys[6], (N_TM, N_USER, N_USER, SLOTS), 0, NB_DEV), jax.random.fold_in(arg_keys[6], 1), 0, NB_DEV - 1).astype(jnp.int32)
    tile_slot = draw_tile_slot(jax.random.fold_in(arg_keys[10], 71), 0)
    tile_item = plant(ranked_ids(arg_keys[8], (N_TM, N_USER, NT_CAP), ITEM_TILES, 2), jax.random.fold_in(arg_keys[8], 3), 0, ITEM_TILES - 1).astype(jnp.int32)
    tile_count = draw_tile_count(jax.random.fold_in(arg_keys[10], 71), 0)
    return {"user_factor": user_factor, "user_tangent": user_tangent, "item_factor": item_factor, "item_tangent": item_tangent, "time_factor": time_factor, "time_tangent": time_tangent, "send_list": send_list, "tile_slot": tile_slot, "tile_item": tile_item, "tile_count": tile_count}


OBS_WEIGHT = 0.03125
LAMBDA_USER = 0.5
LAMBDA_ITEM = 0.5
LAMBDA_TIME = 1.0


def round_half(values):
    return lax.optimization_barrier(values.astype(jnp.bfloat16)).astype(jnp.float32)


def reference(user_factor, user_tangent, item_factor, item_tangent, time_factor, time_tangent, send_list, tile_slot, tile_item, tile_count):
    shards = jnp.arange(N_TM, dtype=jnp.int32)[:, None] * jnp.ones((1, N_USER), jnp.int32)
    groups = jnp.ones((N_TM, 1), jnp.int32) * jnp.arange(N_USER, dtype=jnp.int32)[None, :]
    user_blocks = user_factor.reshape(N_USER * NB_DEV, UB, R)
    user_deltas = user_tangent.reshape(N_USER * NB_DEV, UB, R)
    item_tiles = item_factor.reshape(ITEM_TILES, IT, R)
    item_deltas = item_tangent.reshape(ITEM_TILES, IT, R)
    time_rows = time_factor.astype(jnp.float32).reshape(N_TM, 1, TS, 1, R)
    time_delta = time_tangent.astype(jnp.float32).reshape(N_TM, 1, TS, 1, R)

    def advance(carry, number):
        user_acc, item_acc, time_acc = carry
        where = tile_slot[:, :, number]
        sender = where // SLOTS
        local = send_list[shards, sender, groups, where % SLOTS]
        block = (sender * NB_DEV + local).astype(jnp.int32)
        which = tile_item[:, :, number]
        weight = OBS_WEIGHT * (number < tile_count).astype(jnp.float32)
        factor_u = user_blocks[block].astype(jnp.float32)[:, :, None]
        delta_u = user_deltas[block].astype(jnp.float32)[:, :, None]
        factor_v = item_tiles[which].astype(jnp.float32)
        delta_v = item_deltas[which].astype(jnp.float32)
        scaled = round_half(factor_u * time_rows)
        mixed = round_half(delta_u * time_rows + factor_u * time_delta)
        change = round_half(jnp.einsum("ajtur,ajir->ajtui", mixed, factor_v) + jnp.einsum("ajtur,ajir->ajtui", scaled, delta_v))
        projected = jnp.einsum("ajtui,ajir->ajtur", change, factor_v)
        user_term = jnp.sum(projected * time_rows, axis=2) * weight[:, :, None, None]
        time_term = jnp.sum(projected * factor_u, axis=3) * weight[:, :, None, None]
        item_term = jnp.einsum("ajtui,ajtur->ajir", change, scaled) * weight[:, :, None, None]
        user_acc = user_acc.at[block.reshape(-1)].add(user_term.reshape(-1, UB, R))
        item_acc = item_acc.at[which.reshape(-1)].add(item_term.reshape(-1, IT, R))
        time_acc = time_acc + jnp.sum(time_term, axis=1)
        return (user_acc, item_acc, time_acc), None

    start = (jnp.zeros((N_USER * NB_DEV, UB, R), jnp.float32), jnp.zeros((ITEM_TILES, IT, R), jnp.float32), jnp.zeros((N_TM, TS, R), jnp.float32))
    (user_acc, item_acc, time_acc), unused = lax.scan(advance, start, jnp.arange(NT_CAP, dtype=jnp.int32))
    delta_time = time_tangent.astype(jnp.float32)
    second = delta_time[:-2] - 2.0 * delta_time[1:-1] + delta_time[2:]
    penalty = jnp.zeros_like(delta_time).at[:-2].add(second).at[1:-1].add(-2.0 * second).at[2:].add(second)
    user_hvp = user_acc.reshape(USERS, R) + LAMBDA_USER * user_tangent.astype(jnp.float32)
    item_hvp = item_acc.reshape(ITEMS, R) + LAMBDA_ITEM * item_tangent.astype(jnp.float32)
    time_hvp = time_acc.reshape(STEPS, R) + LAMBDA_TIME * penalty
    return (user_hvp, item_hvp, time_hvp)
```

```python
import functools

import jax
import jax.numpy as jnp
from jax import lax
from jax.experimental import pallas as pl
from jax.experimental.pallas import tpu as pltpu
from jax.sharding import PartitionSpec as P

R = 128
UB = 128
IT = 256
LANES = 128

OBS_WEIGHT = 0.03125
LAMBDA_USER = 0.5
LAMBDA_ITEM = 0.5
LAMBDA_TIME = 1.0

F32 = jnp.float32
BF16 = jnp.bfloat16
VM = pl.BlockSpec(memory_space=pltpu.VMEM)
SM = pl.BlockSpec(memory_space=pltpu.SMEM)


def iota(shape, dim):
    return lax.broadcasted_iota(jnp.int32, shape, dim)


def dot_tn(left, right):
    return lax.dot_general(left, right, (((0,), (0,)), ((), ())), preferred_element_type=F32)


def dot_nn(left, right):
    return lax.dot_general(left, right, (((1,), (0,)), ((), ())), preferred_element_type=F32)


def halves(values):
    high = values.astype(BF16)
    return high, (values - high.astype(F32)).astype(BF16)


def dot_split(left, right):
    both = dot_nn(left, jnp.concatenate(halves(right), axis=1))
    width = right.shape[1]
    return both[:, :width] + both[:, width:]


def pack_kernel(dims, v_ref, dv_ref, w_ref, dw_ref, send_ref, slot_ref, item_ref, count_ref, out_ref, time_ref):
    tm, peers, tiles, steps, rows = dims
    me = lax.axis_index("user")
    part = rows // peers
    start = pl.multiple_of(me * part, part)
    out_ref[0:part, :] = v_ref[pl.ds(start, part), :]
    out_ref[part : 2 * part, :] = dv_ref[pl.ds(start, part), :]
    time_ref[0:steps, :] = w_ref[...].astype(F32)
    time_ref[steps:, :] = dw_ref[...].astype(F32)
    piece = 2 * steps // peers
    time_rows = time_ref[pl.ds(pl.multiple_of(me * piece, piece), piece), :]
    slots = send_ref.shape[3]
    row, lane = iota((8, LANES), 0), iota((8, LANES), 1)
    wanted = row * slots + lane % slots
    table = jnp.full((8, LANES), -1, jnp.int32)
    count = count_ref[0, 0]
    for n in range(slot_ref.shape[2]):
        hit = (wanted == slot_ref[0, 0, n]) & (n < count)
        table = jnp.where(hit, item_ref[0, 0, n], table)
    entry = lane % (peers * slots)
    for j in range(peers):
        for s in range(slots):
            table = jnp.where((row == peers) & (entry == j * slots + s), send_ref[0, 0, j, s], table)
    out_ref[2 * part :, :] = jnp.concatenate([time_rows, table.astype(F32)], axis=0).astype(BF16)


def gram_kernel(u_ref, du_ref, out_ref):
    def one(g, carry):
        at = pl.ds(pl.multiple_of(g * UB, UB), UB)
        u = u_ref[at, :]
        out_ref[g] = dot_tn(jnp.concatenate([u, du_ref[at, :]], axis=1), u)
        return carry

    lax.fori_loop(0, out_ref.shape[0], one, 0)


def weighted(table, wt, ww):
    high, low = halves(wt * table)
    return dot_nn(jnp.concatenate([high, low], axis=1), ww)


def partial_kernel(dims, got_ref, gram_ref, v_ref, dv_ref, w_ref, dw_ref, out_ref, wt_ref, ww_ref, gh_ref, c_ref, own_ref):
    tm, peers, tiles, steps, rows = dims
    blocks = gram_ref.shape[0]
    part = rows // peers
    piece = 2 * steps // peers
    entries = LANES // steps
    chunks = tm // entries
    me_tm, me = lax.axis_index("tm"), lax.axis_index("user")
    lane, row8 = iota((8, LANES), 1), iota((8, LANES), 0)
    slots = steps // peers

    owner = iota((LANES, LANES), 0) // steps
    spread = (owner == iota((LANES, LANES), 1) // steps).astype(BF16)
    coeff_rows = me_tm * steps + iota((steps, LANES), 0)
    penalty = jnp.zeros((steps, R), F32)
    total_steps = tm * steps
    for chunk in range(chunks):
        base = chunk * entries
        pieces = []
        found_m = jnp.zeros((8, LANES), F32)
        found_g = jnp.zeros((8, LANES), F32)
        for a in range(entries):
            for j in range(peers):
                tile = got_ref[(base + a) * peers + j, 2 * part :, :].astype(F32)
                pieces.append(tile[:piece])
                mine = lane // steps == a
                hit = mine & (row8 == me) & (lane // slots % peers == j)
                found_m = found_m + jnp.where(hit, tile[piece:], 0.0)
                hit = mine & (row8 == peers) & (me == j)
                found_g = found_g + jnp.where(hit, tile[piece:], 0.0)
        half = peers // 2
        w = jnp.concatenate([pieces[a * peers + j] for a in range(entries) for j in range(half)], axis=0)
        dw = jnp.concatenate([pieces[a * peers + j] for a in range(entries) for j in range(half, peers)], axis=0)
        ww = w.astype(BF16)
        wt_ref[chunk] = jnp.concatenate([w, dw], axis=1).T
        ww_ref[chunk] = jnp.concatenate([ww, ww], axis=0)
        item = jnp.sum(found_m, axis=0, keepdims=True)
        block = jnp.sum(found_g, axis=0, keepdims=True)
        number = jnp.where(item < 0.0, -1.0, block * tiles + item).astype(jnp.int32)
        hot = (iota((blocks * tiles, LANES), 0) == number).astype(BF16)
        mine = (owner == me_tm - base).astype(BF16)
        counts = dot_nn(hot, jnp.concatenate([spread, mine], axis=1))
        c_ref[chunk] = counts[:, :LANES]
        own_ref[...] = counts[:, LANES:] + (own_ref[...] if chunk else 0.0)
        column = chunk * LANES + iota((steps, LANES), 1)
        coeff = jnp.zeros((steps, LANES), F32)
        for shift, scale in ((-1, 1.0), (0, -2.0), (1, 1.0)):
            centre = coeff_rows + shift
            inside = (centre >= 1) & (centre <= total_steps - 2)
            apart = column - centre
            value = jnp.where(apart == 0, -2.0, jnp.where(jnp.abs(apart) == 1, 1.0, 0.0))
            coeff = coeff + jnp.where(inside, scale * value, 0.0)
        penalty = penalty + dot_nn(coeff.astype(BF16), dw.astype(BF16))

    per_tile = IT // rows

    def item_grams(m, carry):
        def gathered(first):
            return jnp.concatenate(
                [got_ref[(m * per_tile + a) * peers + j, first : first + part, :] for a in range(per_tile) for j in range(peers)],
                axis=0,
            )

        v = gathered(0)
        gh_ref[m] = dot_tn(jnp.concatenate([v, gathered(part)], axis=1), v)
        return carry

    lax.fori_loop(0, tiles, item_grams, 0, unroll=tiles <= 2)

    def time_terms(m, carry):
        def add(g, total):
            return total + own_ref[pl.ds(g * tiles + m, 1), :] * gram_ref[g]

        total = lax.fori_loop(0, blocks, add, jnp.zeros((2 * R, R), F32), unroll=4)
        s, d = total[:R], total[R:]
        g_m, h_m = gh_ref[m, :R], gh_ref[m, R:]
        q, r = carry
        return q + d * g_m + s * h_m, r + s * g_m

    zero = jnp.zeros((R, R), F32)
    q, r = lax.fori_loop(0, tiles, time_terms, (zero, zero), unroll=tiles <= 2)
    left = jnp.concatenate([w_ref[...], dw_ref[...]], axis=1)
    time_rows = OBS_WEIGHT * dot_split(left, jnp.concatenate([q, r], axis=0))

    my_tile = me_tm * rows // IT

    def item_terms(g, carry):
        s, d = gram_ref[g, :R], gram_ref[g, R:]
        both = jnp.zeros((2 * R, R), F32)
        for chunk in range(chunks):
            both = both + weighted(c_ref[chunk, pl.ds(g * tiles + my_tile, 1), :], wt_ref[chunk], ww_ref[chunk])
        y, z = both[:R], both[R:]
        a, b = carry
        return a + d * y + s * z, b + s * y

    a, b = lax.fori_loop(0, blocks, item_terms, (zero, zero), unroll=2)
    left = jnp.concatenate([v_ref[...], dv_ref[...]], axis=1)
    item_rows = OBS_WEIGHT * dot_split(left, jnp.concatenate([a, b], axis=0))

    first = jnp.where(me == 0, 1.0, 0.0)
    out_ref[:rows, :] = item_rows + (first * LAMBDA_ITEM) * dv_ref[...].astype(F32)
    out_ref[rows:, :] = time_rows + (first * LAMBDA_TIME) * penalty


def user_kernel(dims, u_ref, du_ref, wt_ref, ww_ref, gh_ref, c_ref, out_ref):
    tm, peers, tiles, steps, rows = dims
    chunks = wt_ref.shape[0]

    def one(g, carry):
        def add(m, total):
            both = jnp.zeros((2 * R, R), F32)
            for chunk in range(chunks):
                both = both + weighted(c_ref[chunk, pl.ds(g * tiles + m, 1), :], wt_ref[chunk], ww_ref[chunk])
            y, z = both[:R], both[R:]
            g_m, h_m = gh_ref[m, :R], gh_ref[m, R:]
            return total[0] + g_m * y, total[1] + g_m * z + h_m * y

        zero = jnp.zeros((R, R), F32)
        k_delta, k_factor = lax.fori_loop(0, tiles, add, (zero, zero), unroll=tiles <= 2)
        at = pl.ds(pl.multiple_of(g * UB, UB), UB)
        du = du_ref[at, :]
        left = jnp.concatenate([du, u_ref[at, :]], axis=1)
        term = dot_split(left, jnp.concatenate([k_delta, k_factor], axis=0))
        out_ref[at, :] = OBS_WEIGHT * term + LAMBDA_USER * du.astype(F32)
        return carry

    lax.fori_loop(0, out_ref.shape[0] // UB, one, 0)


def shape(dims, dtype=F32):
    return jax.ShapeDtypeStruct(dims, dtype)


def body(user_factor, user_tangent, item_factor, item_tangent, time_factor, time_tangent, send_list, tile_slot, tile_item, tile_count):
    tm, peers = lax.axis_size("tm"), lax.axis_size("user")
    rows, steps = item_factor.shape[0], time_factor.shape[0]
    tiles = rows * tm // IT
    blocks = user_factor.shape[0] // UB
    dims = (tm, peers, tiles, steps, rows)
    chunks = tm * steps // LANES
    height = 2 * rows // peers + 2 * steps // peers + 8
    packed = pl.pallas_call(
        functools.partial(pack_kernel, dims),
        out_shape=shape((height, R), BF16),
        in_specs=[VM] * 4 + [SM] * 4,
        out_specs=VM,
        scratch_shapes=[pltpu.VMEM((2 * steps, R), F32)],
        name="pack",
    )(item_factor, item_tangent, time_factor, time_tangent, send_list, tile_slot, tile_item, tile_count)
    grams = pl.pallas_call(
        gram_kernel, out_shape=shape((blocks, 2 * R, R)), in_specs=[VM] * 2, out_specs=VM, name="grams"
    )(user_factor, user_tangent)
    got = lax.all_to_all(
        jnp.broadcast_to(packed[None], (tm * peers, height, R)), ("tm", "user"), split_axis=0, concat_axis=0, tiled=True
    )
    partial, wt, ww, gh, counts, _ = pl.pallas_call(
        functools.partial(partial_kernel, dims),
        out_shape=(
            shape((rows + steps, R)),
            shape((chunks, 2 * R, LANES)),
            shape((chunks, 2 * LANES, R), BF16),
            shape((tiles, 2 * R, R)),
            shape((chunks, blocks * tiles, LANES)),
            shape((blocks * tiles, LANES)),
        ),
        in_specs=[VM] * 6,
        out_specs=(VM,) * 6,
        name="partials",
    )(got, grams, item_factor, item_tangent, time_factor, time_tangent)
    step = 1
    while step < peers:
        partial = partial + lax.ppermute(partial, "user", [(i, i ^ step) for i in range(peers)])
        step *= 2
    user_hvp = pl.pallas_call(
        functools.partial(user_kernel, dims),
        out_shape=shape(user_factor.shape),
        in_specs=[VM] * 6,
        out_specs=VM,
        name="user_rows",
    )(user_factor, user_tangent, wt, ww, gh, counts)
    return (user_hvp, partial[:rows], partial[rows:])


def solution(mesh):
    return jax.shard_map(
        body,
        mesh=mesh,
        in_specs=(
            P("user", None),
            P("user", None),
            P("tm", None),
            P("tm", None),
            P("tm", None),
            P("tm", None),
            P("tm", "user", None, None),
            P("tm", "user", None),
            P("tm", "user", None),
            P("tm", "user"),
        ),
        out_specs=(P("user", None), P("tm", None), P("tm", None)),
        check_vma=False,
    )
```

```python
import functools

import jax
import jax.numpy as jnp
from jax import lax
from jax.experimental import pallas as pl
from jax.experimental.pallas import tpu as pltpu
from jax.sharding import PartitionSpec as P

R = 128
UB = 128
IT = 256
LANES = 128

OBS_WEIGHT = 0.03125
LAMBDA_USER = 0.5
LAMBDA_ITEM = 0.5
LAMBDA_TIME = 1.0

F32 = jnp.float32
BF16 = jnp.bfloat16
VM = pl.BlockSpec(memory_space=pltpu.VMEM)
SM = pl.BlockSpec(memory_space=pltpu.SMEM)


def iota(shape, dim):
    return lax.broadcasted_iota(jnp.int32, shape, dim)


def dot_tn(left, right):
    return lax.dot_general(left, right, (((0,), (0,)), ((), ())), preferred_element_type=F32)


def dot_nn(left, right):
    return lax.dot_general(left, right, (((1,), (0,)), ((), ())), preferred_element_type=F32)


def halves(values):
    high = values.astype(BF16)
    return high, (values - high.astype(F32)).astype(BF16)


def dot_split(left, right):
    both = dot_nn(left, jnp.concatenate(halves(right), axis=1))
    width = right.shape[1]
    return both[:, :width] + both[:, width:]


def pack_kernel(dims, v_ref, dv_ref, w_ref, dw_ref, send_ref, slot_ref, item_ref, count_ref, out_ref, time_ref):
    tm, peers, tiles, steps, rows = dims
    me = lax.axis_index("user")
    part = rows // peers
    start = pl.multiple_of(me * part, part)
    time_ref[0:steps, :] = w_ref[...].astype(F32)
    time_ref[steps:, :] = dw_ref[...].astype(F32)
    piece = 2 * steps // peers
    time_rows = time_ref[pl.ds(pl.multiple_of(me * piece, piece), piece), :]
    slots = send_ref.shape[3]
    row, lane = iota((8, LANES), 0), iota((8, LANES), 1)
    wanted = row * slots + lane % slots
    table = jnp.full((8, LANES), -1, jnp.int32)
    count = count_ref[0]
    for n in range(slot_ref.shape[2]):
        hit = (wanted == slot_ref[0, 0, n]) & (n < count)
        table = jnp.where(hit, item_ref[0, 0, n], table)
    entry = lane % (peers * slots)
    for j in range(peers):
        for s in range(slots):
            table = jnp.where((row == peers) & (entry == j * slots + s), send_ref[0, 0, j, s], table)
    last = jnp.concatenate([time_rows, table.astype(F32)], axis=0).astype(BF16)
    whole = jnp.concatenate([v_ref[pl.ds(start, part), :], dv_ref[pl.ds(start, part), :], last], axis=0)
    out_ref[...] = jnp.broadcast_to(whole[None], out_ref.shape)


def gram_kernel(u_ref, du_ref, out_ref):
    def one(g, carry):
        at = pl.ds(pl.multiple_of(g * UB, UB), UB)
        u = u_ref[at, :]
        out_ref[g] = dot_tn(jnp.concatenate([u, du_ref[at, :]], axis=1), u)
        return carry

    lax.fori_loop(0, out_ref.shape[0], one, 0, unroll=4)


def weighted(table, wt, ww):
    high, low = halves(wt * table)
    return dot_nn(jnp.concatenate([high, low], axis=1), ww)


def partial_kernel(dims, got_ref, gram_ref, v_ref, dv_ref, w_ref, dw_ref, out_ref, wt_ref, ww_ref, gh_ref, c_ref, own_ref):
    tm, peers, tiles, steps, rows = dims
    blocks = gram_ref.shape[0]
    part = rows // peers
    piece = 2 * steps // peers
    entries = LANES // steps
    chunks = tm // entries
    me_tm, me = lax.axis_index("tm"), lax.axis_index("user")
    lane, row8 = iota((8, LANES), 1), iota((8, LANES), 0)
    slots = steps // peers

    owner = iota((LANES, LANES), 0) // steps
    spread = (owner == iota((LANES, LANES), 1) // steps).astype(BF16)
    coeff_rows = me_tm * steps + iota((steps, LANES), 0)
    penalty = jnp.zeros((steps, R), F32)
    total_steps = tm * steps
    for chunk in range(chunks):
        base = chunk * entries
        pieces = []
        found_m = jnp.zeros((8, LANES), F32)
        found_g = jnp.zeros((8, LANES), F32)
        for a in range(entries):
            for j in range(peers):
                tile = got_ref[(base + a) * peers + j, 2 * part :, :].astype(F32)
                pieces.append(tile[:piece])
                mine = lane // steps == a
                hit = mine & (row8 == me) & (lane // slots % peers == j)
                found_m = found_m + jnp.where(hit, tile[piece:], 0.0)
                hit = mine & (row8 == peers) & (me == j)
                found_g = found_g + jnp.where(hit, tile[piece:], 0.0)
        half = peers // 2
        w = jnp.concatenate([pieces[a * peers + j] for a in range(entries) for j in range(half)], axis=0)
        dw = jnp.concatenate([pieces[a * peers + j] for a in range(entries) for j in range(half, peers)], axis=0)
        ww = w.astype(BF16)
        wt_ref[chunk] = jnp.concatenate([w, dw], axis=1).T
        ww_ref[chunk] = jnp.concatenate([ww, ww], axis=0)
        item = jnp.sum(found_m, axis=0, keepdims=True)
        block = jnp.sum(found_g, axis=0, keepdims=True)
        number = jnp.where(item < 0.0, -1.0, block * tiles + item).astype(jnp.int32)
        hot = (iota((blocks * tiles, LANES), 0) == number).astype(BF16)
        mine = (owner == me_tm - base).astype(BF16)
        counts = dot_nn(hot, jnp.concatenate([spread, mine], axis=1))
        c_ref[chunk] = counts[:, :LANES]
        own_ref[...] = counts[:, LANES:] + (own_ref[...] if chunk else 0.0)
        column = chunk * LANES + iota((steps, LANES), 1)
        coeff = jnp.zeros((steps, LANES), F32)
        for shift, scale in ((-1, 1.0), (0, -2.0), (1, 1.0)):
            centre = coeff_rows + shift
            inside = (centre >= 1) & (centre <= total_steps - 2)
            apart = column - centre
            value = jnp.where(apart == 0, -2.0, jnp.where(jnp.abs(apart) == 1, 1.0, 0.0))
            coeff = coeff + jnp.where(inside, scale * value, 0.0)
        penalty = penalty + dot_nn(coeff.astype(BF16), dw.astype(BF16))

    per_tile = IT // rows

    def item_grams(m, carry):
        def gathered(first):
            return jnp.concatenate(
                [got_ref[(m * per_tile + a) * peers + j, first : first + part, :] for a in range(per_tile) for j in range(peers)],
                axis=0,
            )

        v = gathered(0)
        gh_ref[m] = dot_tn(jnp.concatenate([v, gathered(part)], axis=1), v)
        return carry

    lax.fori_loop(0, tiles, item_grams, 0, unroll=tiles <= 2)

    def time_terms(m, carry):
        def add(g, total):
            return total + own_ref[pl.ds(g * tiles + m, 1), :] * gram_ref[g]

        total = lax.fori_loop(0, blocks, add, jnp.zeros((2 * R, R), F32), unroll=4)
        s, d = total[:R], total[R:]
        g_m, h_m = gh_ref[m, :R], gh_ref[m, R:]
        q, r = carry
        return q + d * g_m + s * h_m, r + s * g_m

    zero = jnp.zeros((R, R), F32)
    q, r = lax.fori_loop(0, tiles, time_terms, (zero, zero), unroll=tiles <= 2)
    left = jnp.concatenate([w_ref[...], dw_ref[...]], axis=1)
    time_rows = OBS_WEIGHT * dot_split(left, jnp.concatenate([q, r], axis=0))

    my_tile = me_tm * rows // IT

    def item_terms(g, carry):
        s, d = gram_ref[g, :R], gram_ref[g, R:]
        both = jnp.zeros((2 * R, R), F32)
        for chunk in range(chunks):
            both = both + weighted(c_ref[chunk, pl.ds(g * tiles + my_tile, 1), :], wt_ref[chunk], ww_ref[chunk])
        y, z = both[:R], both[R:]
        a, b = carry
        return a + d * y + s * z, b + s * y

    a, b = lax.fori_loop(0, blocks, item_terms, (zero, zero), unroll=4)
    left = jnp.concatenate([v_ref[...], dv_ref[...]], axis=1)
    item_rows = OBS_WEIGHT * dot_split(left, jnp.concatenate([a, b], axis=0))

    first = jnp.where(me == 0, 1.0, 0.0)
    out_ref[:rows, :] = item_rows + (first * LAMBDA_ITEM) * dv_ref[...].astype(F32)
    out_ref[rows:, :] = time_rows + (first * LAMBDA_TIME) * penalty


def user_kernel(dims, u_ref, du_ref, wt_ref, ww_ref, gh_ref, c_ref, out_ref):
    tm, peers, tiles, steps, rows = dims
    chunks = wt_ref.shape[0]

    def one(g, carry):
        def add(m, total):
            both = jnp.zeros((2 * R, R), F32)
            for chunk in range(chunks):
                both = both + weighted(c_ref[chunk, pl.ds(g * tiles + m, 1), :], wt_ref[chunk], ww_ref[chunk])
            y, z = both[:R], both[R:]
            g_m, h_m = gh_ref[m, :R], gh_ref[m, R:]
            return total[0] + g_m * y, total[1] + g_m * z + h_m * y

        zero = jnp.zeros((R, R), F32)
        k_delta, k_factor = lax.fori_loop(0, tiles, add, (zero, zero), unroll=tiles <= 2)
        at = pl.ds(pl.multiple_of(g * UB, UB), UB)
        du = du_ref[at, :]
        left = jnp.concatenate([du, u_ref[at, :]], axis=1)
        term = dot_split(left, jnp.concatenate([k_delta, k_factor], axis=0))
        out_ref[at, :] = OBS_WEIGHT * term + LAMBDA_USER * du.astype(F32)
        return carry

    lax.fori_loop(0, out_ref.shape[0] // UB, one, 0, unroll=4)


def finish_kernel(rows, *refs):
    item_ref, time_ref = refs[-2:]
    item_ref[...] = functools.reduce(jnp.add, [ref[:rows, :] for ref in refs[:-2]])
    time_ref[...] = functools.reduce(jnp.add, [ref[rows:, :] for ref in refs[:-2]])


def shape(dims, dtype=F32):
    return jax.ShapeDtypeStruct(dims, dtype)


def placed(small):
    if not small:
        return shape, lambda *arrays: arrays
    return pltpu.VMEM, lambda *arrays: [pltpu.with_memory_space_constraint(x, pltpu.VMEM) for x in arrays]


def body(user_factor, user_tangent, item_factor, item_tangent, time_factor, time_tangent, send_list, tile_slot, tile_item, tile_count):
    tm, peers = lax.axis_size("tm"), lax.axis_size("user")
    rows, steps = item_factor.shape[0], time_factor.shape[0]
    tiles = rows * tm // IT
    blocks = user_factor.shape[0] // UB
    dims = (tm, peers, tiles, steps, rows)
    chunks = tm * steps // LANES
    near, held = placed(chunks == 1 and tiles <= 2)
    height = 2 * rows // peers + 2 * steps // peers + 8
    packed = pl.pallas_call(
        functools.partial(pack_kernel, dims),
        out_shape=near((tm * peers, height, R), BF16),
        in_specs=[VM] * 4 + [SM] * 4,
        out_specs=VM,
        scratch_shapes=[pltpu.VMEM((2 * steps, R), F32)],
        name="pack",
    )(item_factor, item_tangent, time_factor, time_tangent, send_list, tile_slot, tile_item, tile_count.reshape(1))
    grams = pl.pallas_call(
        gram_kernel, out_shape=near((blocks, 2 * R, R), F32), in_specs=[VM] * 2, out_specs=VM, name="grams"
    )(user_factor, user_tangent)
    got = lax.all_to_all(
        packed, ("tm", "user"), split_axis=0, concat_axis=0, tiled=True
    )
    partial, wt, ww, gh, counts, _ = pl.pallas_call(
        functools.partial(partial_kernel, dims),
        out_shape=(
            near((rows + steps, R), F32),
            near((chunks, 2 * R, LANES), F32),
            near((chunks, 2 * LANES, R), BF16),
            near((tiles, 2 * R, R), F32),
            near((chunks, blocks * tiles, LANES), F32),
            near((blocks * tiles, LANES), F32),
        ),
        in_specs=[VM] * 6,
        out_specs=(VM,) * 6,
        name="partials",
    )(*held(got, grams), item_factor, item_tangent, time_factor, time_tangent)
    others = [lax.ppermute(partial, "user", [(i, (i + d) % peers) for i in range(peers)]) for d in range(1, peers)]
    user_hvp = pl.pallas_call(
        functools.partial(user_kernel, dims),
        out_shape=shape(user_factor.shape),
        in_specs=[VM] * 6,
        out_specs=VM,
        name="user_rows",
    )(user_factor, user_tangent, *held(wt, ww, gh, counts))
    item_hvp, time_hvp = pl.pallas_call(
        functools.partial(finish_kernel, rows),
        out_shape=(shape((rows, R)), shape((steps, R))),
        in_specs=[VM] * peers,
        out_specs=(VM, VM),
        name="finish",
    )(*held(partial), *held(*others))
    return (user_hvp, item_hvp, time_hvp)


def solution(mesh):
    return jax.shard_map(
        body,
        mesh=mesh,
        in_specs=(
            P("user", None),
            P("user", None),
            P("tm", None),
            P("tm", None),
            P("tm", None),
            P("tm", None),
            P("tm", "user", None, None),
            P("tm", "user", None),
            P("tm", "user", None),
            P("tm", "user"),
        ),
        out_specs=(P("user", None), P("tm", None), P("tm", None)),
        check_vma=False,
    )
```

```python
import functools

import jax
import jax.numpy as jnp
from jax import lax
from jax.experimental import pallas as pl
from jax.experimental.pallas import tpu as pltpu
from jax.sharding import PartitionSpec as P

R = 128
UB = 128
IT = 256
LANES = 128
SUB = 8

OBS_WEIGHT = 0.03125
LAMBDA_USER = 0.5
LAMBDA_ITEM = 0.5
LAMBDA_TIME = 1.0

F32 = jnp.float32
BF16 = jnp.bfloat16
VM = pl.BlockSpec(memory_space=pltpu.VMEM)
HBM = pl.BlockSpec(memory_space=pltpu.HBM)
SM = pl.BlockSpec(memory_space=pltpu.SMEM)


def iota(shape, dim):
    return lax.broadcasted_iota(jnp.int32, shape, dim)


def dot_tn(left, right):
    return lax.dot_general(left, right, (((0,), (0,)), ((), ())), preferred_element_type=F32)


def dot_nn(left, right):
    return lax.dot_general(left, right, (((1,), (0,)), ((), ())), preferred_element_type=F32)


def halves(values):
    high = values.astype(BF16)
    return high, (values - high.astype(F32)).astype(BF16)


def dot_split(left, right):
    both = dot_nn(left, jnp.concatenate(halves(right), axis=1))
    width = right.shape[1]
    return both[:, :width] + both[:, width:]


def pack_kernel(dims, v_ref, dv_ref, w_ref, dw_ref, send_ref, slot_ref, item_ref, count_ref, out_ref, time_ref):
    tm, peers, tiles, steps, rows = dims
    me = lax.axis_index("user")
    part = rows // peers
    start = pl.multiple_of(me * part, part)
    time_ref[0:steps, :] = w_ref[...].astype(F32)
    time_ref[steps:, :] = dw_ref[...].astype(F32)
    piece = 2 * steps // peers
    time_rows = time_ref[pl.ds(pl.multiple_of(me * piece, piece), piece), :]
    slots = send_ref.shape[3]
    row, lane = iota((8, LANES), 0), iota((8, LANES), 1)
    wanted = row * slots + lane % slots
    table = jnp.full((8, LANES), -1, jnp.int32)
    count = count_ref[0]
    for n in range(slot_ref.shape[2]):
        hit = (wanted == slot_ref[0, 0, n]) & (n < count)
        table = jnp.where(hit, item_ref[0, 0, n], table)
    entry = lane % (peers * slots)
    for j in range(peers):
        for s in range(slots):
            table = jnp.where((row == peers) & (entry == j * slots + s), send_ref[0, 0, j, s], table)
    last = jnp.concatenate([time_rows, table.astype(F32)], axis=0).astype(BF16)
    whole = jnp.concatenate([v_ref[pl.ds(start, part), :], dv_ref[pl.ds(start, part), :], last], axis=0)
    out_ref[...] = jnp.broadcast_to(whole[None], out_ref.shape)


def gram_kernel(u_ref, du_ref, out_ref):
    blocks = u_ref.shape[0] // UB
    groups = R // SUB

    def pair(i, carry):
        sides = []
        for g in (2 * i, 2 * i + 1):
            at = pl.ds(pl.multiple_of(g * UB, UB), UB)
            u = u_ref[at, :]
            gram = dot_tn(jnp.concatenate([u, du_ref[at, :]], axis=1), u)
            sides.append(jnp.concatenate([gram[:R], gram[R:]], axis=1).reshape(groups, SUB, 2 * R))
        high, low = halves(jnp.concatenate(sides, axis=1))
        at = pl.multiple_of(i * 2 * SUB, 2 * SUB)
        out_ref[:, pl.ds(at, 2 * SUB), :] = high
        out_ref[:, pl.ds(at + blocks * SUB, 2 * SUB), :] = low
        return carry

    lax.fori_loop(0, blocks // 2, pair, 0, unroll=2)


def dot_nt(left, right):
    return lax.dot_general(left, right, (((1,), (1,)), ((), ())), preferred_element_type=F32)


def count_rows(left, right, keep):
    counts = dot_nt(left.astype(BF16), right.astype(BF16))
    same = iota(counts.shape, 0) % SUB == iota(counts.shape, 1) % SUB
    counts = jnp.where(same, counts, 0.0).astype(BF16)
    return jnp.concatenate([counts, counts], axis=1) if keep else counts


def time_grams(wt, w, out_ref, at, steps):
    owner = iota((LANES, R), 0) // steps
    zero = jnp.zeros((LANES, R), BF16)
    for a in range(0, LANES // steps, 2):
        right = jnp.concatenate([jnp.where(owner == a + i, w, zero) for i in range(2)], axis=1)
        both = dot_nn(wt, right)
        out_ref[at + a] = both[:, :R]
        out_ref[at + a + 1] = both[:, R:]


def partial_kernel(dims, got_ref, gram_ref, v_ref, dv_ref, w_ref, dw_ref, out_ref, wt_ref, ww_ref, gh_ref, entry_ref, left_ref, grams_ref):
    tm, peers, tiles, steps, rows = dims
    groups, depth = gram_ref.shape[:2]
    blocks = depth // (2 * SUB)
    part = rows // peers
    piece = 2 * steps // peers
    entries = LANES // steps
    chunks = tm // entries
    me_tm, me = lax.axis_index("tm"), lax.axis_index("user")
    lane, row8 = iota((8, LANES), 1), iota((8, LANES), 0)
    slots = steps // peers
    my_tile = me_tm * rows // IT

    coeff_rows = me_tm * steps + iota((steps, LANES), 0)
    penalty = jnp.zeros((steps, R), F32)
    total_steps = tm * steps
    item_height = entries * SUB
    own_counts = jnp.zeros((tiles * SUB, blocks * SUB), BF16)
    for chunk in range(chunks):
        base = chunk * entries
        pieces = []
        found_m = jnp.zeros((8, LANES), F32)
        found_g = jnp.zeros((8, LANES), F32)
        for a in range(entries):
            for j in range(peers):
                tile = got_ref[(base + a) * peers + j, 2 * part :, :].astype(F32)
                pieces.append(tile[:piece])
                mine = lane // steps == a
                hit = mine & (row8 == me) & (lane // slots % peers == j)
                found_m = found_m + jnp.where(hit, tile[piece:], 0.0)
                hit = mine & (row8 == peers) & (me == j)
                found_g = found_g + jnp.where(hit, tile[piece:], 0.0)
        half = peers // 2
        w = jnp.concatenate([pieces[a * peers + j] for a in range(entries) for j in range(half)], axis=0)
        dw = jnp.concatenate([pieces[a * peers + j] for a in range(entries) for j in range(half, peers)], axis=0)
        wt_ref[chunk] = jnp.concatenate([w, dw], axis=1).T.astype(BF16)
        ww_ref[chunk] = w.astype(BF16)
        time_grams(wt_ref[chunk], ww_ref[chunk], grams_ref, base, steps)
        item = jnp.sum(found_m, axis=0, keepdims=True).astype(jnp.int32)
        block = jnp.sum(found_g, axis=0, keepdims=True).astype(jnp.int32)
        entry_ref[chunk, 0:1, :] = item
        entry_ref[chunk, 1:2, :] = block
        shape_left, shape_right = (item_height, LANES), (blocks * SUB, LANES)
        right = block == iota(shape_right, 0) // SUB
        left = (iota(shape_left, 1) // steps == iota(shape_left, 0) // SUB) & (item == my_tile)
        left_ref[pl.ds(chunk * item_height, item_height), :] = count_rows(left, right, True)
        shape_left = (tiles * SUB, LANES)
        left = (iota(shape_left, 1) // steps == me_tm - base) & (item == iota(shape_left, 0) // SUB)
        own_counts = own_counts + count_rows(left, right, False)
        column = chunk * LANES + iota((steps, LANES), 1)
        coeff = jnp.zeros((steps, LANES), F32)
        for shift, scale in ((-1, 1.0), (0, -2.0), (1, 1.0)):
            centre = coeff_rows + shift
            inside = (centre >= 1) & (centre <= total_steps - 2)
            apart = column - centre
            value = jnp.where(apart == 0, -2.0, jnp.where(jnp.abs(apart) == 1, 1.0, 0.0))
            coeff = coeff + jnp.where(inside, scale * value, 0.0)
        penalty = penalty + dot_nn(coeff.astype(BF16), dw.astype(BF16))
    left_ref[pl.ds(chunks * item_height, tiles * SUB), :] = jnp.concatenate([own_counts, own_counts], axis=1)

    per_tile = IT // rows

    def item_grams(m, carry):
        def gathered(first):
            return jnp.concatenate(
                [got_ref[(m * per_tile + a) * peers + j, first : first + part, :] for a in range(per_tile) for j in range(peers)],
                axis=0,
            )

        v = gathered(0)
        gh_ref[m] = dot_tn(jnp.concatenate([v, gathered(part)], axis=1), v)
        return carry

    lax.fori_loop(0, tiles, item_grams, 0, unroll=tiles <= 2)

    sides = ([], [], [], [])
    for group in range(groups):
        sums = dot_nn(left_ref[...], gram_ref[group])
        s, d = sums[:, :R], sums[:, R:]
        at = pl.ds(group * SUB, SUB)
        below = pl.ds(R + group * SUB, SUB)
        a_rows = b_rows = q_rows = r_rows = jnp.zeros((SUB, R), F32)
        for a in range(tm):
            here = slice(a * SUB, (a + 1) * SUB)
            y, z = grams_ref[a, at, :], grams_ref[a, below, :]
            a_rows = a_rows + d[here] * y + s[here] * z
            b_rows = b_rows + s[here] * y
        for m in range(tiles):
            here = slice((tm + m) * SUB, (tm + m + 1) * SUB)
            g_m, h_m = gh_ref[m, at, :], gh_ref[m, below, :]
            q_rows = q_rows + d[here] * g_m + s[here] * h_m
            r_rows = r_rows + s[here] * g_m
        for side, value in zip(sides, (a_rows, b_rows, q_rows, r_rows)):
            side.append(value)
    left = jnp.concatenate([v_ref[...], dv_ref[...]], axis=1)
    item_rows = OBS_WEIGHT * dot_split(left, jnp.concatenate(sides[0] + sides[1], axis=0))
    left = jnp.concatenate([w_ref[...], dw_ref[...]], axis=1)
    time_rows = OBS_WEIGHT * dot_split(left, jnp.concatenate(sides[2] + sides[3], axis=0))
    first = jnp.where(me == 0, 1.0, 0.0)
    out_ref[:rows, :] = item_rows + (first * LAMBDA_ITEM) * dv_ref[...].astype(F32)
    out_ref[rows:, :] = time_rows + (first * LAMBDA_TIME) * penalty


def user_kernel(dims, u_hbm, du_hbm, wt_ref, ww_ref, gh_ref, entry_ref, out_hbm, u_ref, du_ref, out_ref, grams_ref, k_ref, in_sem, out_sem):
    tm, peers, tiles, steps, rows = dims
    chunks = wt_ref.shape[0]
    entries = LANES // steps
    blocks, groups = k_ref.shape[0], R // SUB
    loads = [
        pltpu.make_async_copy(u_hbm, u_ref, in_sem.at[0]),
        pltpu.make_async_copy(du_hbm, du_ref, in_sem.at[1]),
    ]
    for load in loads:
        load.start()

    width = LANES // (entries * SUB)

    def add(chunk, first, fresh):
        item, block = entry_ref[chunk, 0:1, :], entry_ref[chunk, 1:2, :]
        left = block == iota((blocks * SUB, LANES), 0) // SUB
        shape_right = (entries * width * SUB, LANES)
        place = iota(shape_right, 0) // SUB
        right = (iota(shape_right, 1) // steps == place // width) & (item == first + place % width)
        counts = count_rows(left, right, True)
        for group in range(groups):
            at = pl.ds(group * SUB, SUB)
            below = pl.ds(R + group * SUB, SUB)
            stack = []
            for a in range(entries):
                y, z = grams_ref[a, at, :], grams_ref[a, below, :]
                for m in range(width):
                    g_m, h_m = gh_ref[first + m, at, :], gh_ref[first + m, below, :]
                    stack.append(jnp.concatenate([g_m * y, g_m * z + h_m * y], axis=1))
            high, low = halves(jnp.concatenate(stack, axis=0))
            value = dot_nn(counts, jnp.concatenate([high, low], axis=0)).reshape(blocks, SUB, 2 * R)
            k_ref[:, at, :] = value if fresh else k_ref[:, at, :] + value

    for chunk in range(chunks):
        time_grams(wt_ref[chunk], ww_ref[chunk], grams_ref, 0, steps)
        add(chunk, 0, chunk == 0)

        def rest(i, carry):
            add(chunk, i * width, False)
            return carry

        lax.fori_loop(1, tiles // width, rest, 0)

    for load in loads:
        load.wait()
    stores = []
    per_store = blocks // out_sem.shape[0]
    for number in range(out_sem.shape[0]):
        for g in range(number * per_store, (number + 1) * per_store):
            at = pl.ds(g * UB, UB)
            du = du_ref[at, :]
            left = jnp.concatenate([du, u_ref[at, :]], axis=1)
            term = dot_split(left, jnp.concatenate([k_ref[g, :, :R], k_ref[g, :, R:]], axis=0))
            out_ref[at, :] = OBS_WEIGHT * term + LAMBDA_USER * du.astype(F32)
        at = pl.ds(number * per_store * UB, per_store * UB)
        store = pltpu.make_async_copy(out_ref.at[at, :], out_hbm.at[at, :], out_sem.at[number])
        store.start()
        stores.append(store)
    for store in stores:
        store.wait()


def finish_kernel(rows, *refs):
    item_ref, time_ref = refs[-2:]
    item_ref[...] = functools.reduce(jnp.add, [ref[:rows, :] for ref in refs[:-2]])
    time_ref[...] = functools.reduce(jnp.add, [ref[rows:, :] for ref in refs[:-2]])


def shape(dims, dtype=F32):
    return jax.ShapeDtypeStruct(dims, dtype)


def placed(small):
    if not small:
        return shape, lambda *arrays: arrays
    return pltpu.VMEM, lambda *arrays: [pltpu.with_memory_space_constraint(x, pltpu.VMEM) for x in arrays]


def body(user_factor, user_tangent, item_factor, item_tangent, time_factor, time_tangent, send_list, tile_slot, tile_item, tile_count):
    tm, peers = lax.axis_size("tm"), lax.axis_size("user")
    rows, steps = item_factor.shape[0], time_factor.shape[0]
    tiles = rows * tm // IT
    blocks = user_factor.shape[0] // UB
    dims = (tm, peers, tiles, steps, rows)
    chunks = tm * steps // LANES
    near, held = placed(chunks == 1 and tiles <= 2)
    height = 2 * rows // peers + 2 * steps // peers + 8
    packed = pl.pallas_call(
        functools.partial(pack_kernel, dims),
        out_shape=near((tm * peers, height, R), BF16),
        in_specs=[VM] * 4 + [SM] * 4,
        out_specs=VM,
        scratch_shapes=[pltpu.VMEM((2 * steps, R), F32)],
        name="pack",
    )(item_factor, item_tangent, time_factor, time_tangent, send_list, tile_slot, tile_item, tile_count.reshape(1))
    groups = R // SUB
    grams = pl.pallas_call(
        gram_kernel,
        out_shape=near((groups, 2 * SUB * blocks, 2 * R), BF16),
        in_specs=[VM] * 2,
        out_specs=VM,
        name="grams",
    )(user_factor, user_tangent)
    got = lax.all_to_all(
        packed, ("tm", "user"), split_axis=0, concat_axis=0, tiled=True
    )
    partial, wt, ww, gh, listed = pl.pallas_call(
        functools.partial(partial_kernel, dims),
        out_shape=(
            near((rows + steps, R), F32),
            near((chunks, 2 * R, LANES), BF16),
            near((chunks, LANES, R), BF16),
            near((tiles, 2 * R, R), F32),
            near((chunks, 8, LANES), jnp.int32),
        ),
        in_specs=[VM] * 6,
        out_specs=(VM,) * 5,
        scratch_shapes=[
            pltpu.VMEM(((tm + tiles) * SUB, 2 * SUB * blocks), BF16),
            pltpu.VMEM((tm, 2 * R, R), F32),
        ],
        name="partials",
    )(*held(got, grams), item_factor, item_tangent, time_factor, time_tangent)
    others = [lax.ppermute(partial, "user", [(i, (i + d) % peers) for i in range(peers)]) for d in range(1, peers)]
    user_hvp = pl.pallas_call(
        functools.partial(user_kernel, dims),
        out_shape=shape(user_factor.shape),
        in_specs=[HBM] * 2 + [VM] * 4,
        out_specs=HBM,
        scratch_shapes=[
            pltpu.VMEM(user_factor.shape, BF16),
            pltpu.VMEM(user_factor.shape, BF16),
            pltpu.VMEM(user_factor.shape, F32),
            pltpu.VMEM((LANES // steps, 2 * R, R), F32),
            pltpu.VMEM((blocks, R, 2 * R), F32),
            pltpu.SemaphoreType.DMA((2,)),
            pltpu.SemaphoreType.DMA((4,)),
        ],
        name="user_rows",
    )(user_factor, user_tangent, *held(wt, ww, gh, listed))
    item_hvp, time_hvp = pl.pallas_call(
        functools.partial(finish_kernel, rows),
        out_shape=(shape((rows, R)), shape((steps, R))),
        in_specs=[VM] * peers,
        out_specs=(VM, VM),
        name="finish",
    )(*held(partial), *held(*others))
    return (user_hvp, item_hvp, time_hvp)


def solution(mesh):
    return jax.shard_map(
        body,
        mesh=mesh,
        in_specs=(
            P("user", None),
            P("user", None),
            P("tm", None),
            P("tm", None),
            P("tm", None),
            P("tm", None),
            P("tm", "user", None, None),
            P("tm", "user", None),
            P("tm", "user", None),
            P("tm", "user"),
        ),
        out_specs=(P("user", None), P("tm", None), P("tm", None)),
        check_vma=False,
    )
```

```python
import functools

import jax
import jax.numpy as jnp
from jax import lax
from jax.experimental import pallas as pl
from jax.experimental.pallas import tpu as pltpu
from jax.sharding import PartitionSpec as P

R = 128
UB = 128
IT = 256
LANES = 128
SUB = 8

OBS_WEIGHT = 0.03125
LAMBDA_USER = 0.5
LAMBDA_ITEM = 0.5
LAMBDA_TIME = 1.0

F32 = jnp.float32
BF16 = jnp.bfloat16
VM = pl.BlockSpec(memory_space=pltpu.VMEM)
HBM = pl.BlockSpec(memory_space=pltpu.HBM)
SM = pl.BlockSpec(memory_space=pltpu.SMEM)


def iota(shape, dim):
    return lax.broadcasted_iota(jnp.int32, shape, dim)


def dot_tn(left, right):
    return lax.dot_general(left, right, (((0,), (0,)), ((), ())), preferred_element_type=F32)


def dot_nn(left, right):
    return lax.dot_general(left, right, (((1,), (0,)), ((), ())), preferred_element_type=F32)


def halves(values):
    high = values.astype(BF16)
    return high, (values - high.astype(F32)).astype(BF16)


def dot_split(left, right):
    both = dot_nn(left, jnp.concatenate(halves(right), axis=1))
    width = right.shape[1]
    return both[:, :width] + both[:, width:]


def pack_kernel(dims, v_ref, dv_ref, w_ref, dw_ref, send_ref, slot_ref, item_ref, count_ref, out_ref, time_ref):
    tm, peers, tiles, steps, rows = dims
    me = lax.axis_index("user")
    part = rows // peers
    start = pl.multiple_of(me * part, part)
    time_ref[0:steps, :] = w_ref[...].astype(F32)
    time_ref[steps:, :] = dw_ref[...].astype(F32)
    piece = 2 * steps // peers
    time_rows = time_ref[pl.ds(pl.multiple_of(me * piece, piece), piece), :]
    slots = send_ref.shape[3]
    row, lane = iota((8, LANES), 0), iota((8, LANES), 1)
    wanted = row * slots + lane % slots
    table = jnp.full((8, LANES), -1, jnp.int32)
    count = count_ref[0, 0]
    for n in range(slot_ref.shape[2]):
        hit = (wanted == slot_ref[0, 0, n]) & (n < count)
        table = jnp.where(hit, item_ref[0, 0, n], table)
    entry = lane % (peers * slots)
    for j in range(peers):
        for s in range(slots):
            table = jnp.where((row == peers) & (entry == j * slots + s), send_ref[0, 0, j, s], table)
    last = jnp.concatenate([time_rows, table.astype(F32)], axis=0).astype(BF16)
    whole = jnp.concatenate([v_ref[pl.ds(start, part), :], dv_ref[pl.ds(start, part), :], last], axis=0)
    out_ref[...] = jnp.broadcast_to(whole[None], out_ref.shape)


def gram_kernel(u_ref, du_ref, out_ref):
    blocks = u_ref.shape[0] // UB
    groups = R // SUB

    def pair(i, carry):
        sides = []
        for g in (2 * i, 2 * i + 1):
            at = pl.ds(pl.multiple_of(g * UB, UB), UB)
            u = u_ref[at, :]
            gram = dot_tn(jnp.concatenate([u, du_ref[at, :]], axis=1), u)
            sides.append(jnp.concatenate([gram[:R], gram[R:]], axis=1).reshape(groups, SUB, 2 * R))
        high, low = halves(jnp.concatenate(sides, axis=1))
        at = pl.multiple_of(i * 2 * SUB, 2 * SUB)
        out_ref[:, pl.ds(at, 2 * SUB), :] = high
        out_ref[:, pl.ds(at + blocks * SUB, 2 * SUB), :] = low
        return carry

    lax.fori_loop(0, blocks // 2, pair, 0, unroll=2)


def dot_nt(left, right):
    return lax.dot_general(left, right, (((1,), (1,)), ((), ())), preferred_element_type=F32)


def count_rows(left, right, keep):
    counts = dot_nt(left.astype(BF16), right.astype(BF16))
    same = iota(counts.shape, 0) % SUB == iota(counts.shape, 1) % SUB
    counts = jnp.where(same, counts, 0.0).astype(BF16)
    return jnp.concatenate([counts, counts], axis=1) if keep else counts


def time_grams(wt, w, out_ref, at, steps):
    owner = iota((LANES, R), 0) // steps
    zero = jnp.zeros((LANES, R), BF16)
    for a in range(0, LANES // steps, 2):
        right = jnp.concatenate([jnp.where(owner == a + i, w, zero) for i in range(2)], axis=1)
        both = dot_nn(wt, right)
        out_ref[at + a] = both[:, :R]
        out_ref[at + a + 1] = both[:, R:]


def partial_kernel(dims, got_ref, other_ref, gram_ref, v_ref, dv_ref, w_ref, dw_ref, out_ref, wt_ref, ww_ref, gh_ref, entry_ref, left_ref, grams_ref):
    tm, peers, tiles, steps, rows = dims
    groups, depth = gram_ref.shape[:2]
    blocks = depth // (2 * SUB)
    part = rows // peers
    piece = 2 * steps // peers
    entries = LANES // steps
    chunks = tm // entries
    me_tm, me = lax.axis_index("tm"), lax.axis_index("user")
    lane, row8 = iota((8, LANES), 1), iota((8, LANES), 0)
    slots = steps // peers

    def sent(a, j, first, last):
        here = a * (peers // 2) + j // 2
        return jnp.where(me % 2 == j % 2, got_ref[here, first:last, :], other_ref[here, first:last, :])

    my_tile = me_tm * rows // IT

    coeff_rows = me_tm * steps + iota((steps, LANES), 0)
    penalty = jnp.zeros((steps, R), F32)
    total_steps = tm * steps
    item_height = entries * SUB
    own_counts = jnp.zeros((tiles * SUB, blocks * SUB), BF16)
    for chunk in range(chunks):
        base = chunk * entries
        pieces = []
        found_m = jnp.zeros((8, LANES), F32)
        found_g = jnp.zeros((8, LANES), F32)
        for a in range(entries):
            for j in range(peers):
                tile = sent(base + a, j, 2 * part, 2 * part + 16).astype(F32)
                pieces.append(tile[:piece])
                mine = lane // steps == a
                hit = mine & (row8 == me) & (lane // slots % peers == j)
                found_m = found_m + jnp.where(hit, tile[piece:], 0.0)
                hit = mine & (row8 == peers) & (me == j)
                found_g = found_g + jnp.where(hit, tile[piece:], 0.0)
        half = peers // 2
        w = jnp.concatenate([pieces[a * peers + j] for a in range(entries) for j in range(half)], axis=0)
        dw = jnp.concatenate([pieces[a * peers + j] for a in range(entries) for j in range(half, peers)], axis=0)
        wt_ref[chunk] = jnp.concatenate([w, dw], axis=1).T.astype(BF16)
        ww_ref[chunk] = w.astype(BF16)
        time_grams(wt_ref[chunk], ww_ref[chunk], grams_ref, base, steps)
        item = jnp.sum(found_m, axis=0, keepdims=True).astype(jnp.int32)
        block = jnp.sum(found_g, axis=0, keepdims=True).astype(jnp.int32)
        entry_ref[chunk, 0:1, :] = item
        entry_ref[chunk, 1:2, :] = block
        shape_left, shape_right = (item_height, LANES), (blocks * SUB, LANES)
        right = block == iota(shape_right, 0) // SUB
        left = (iota(shape_left, 1) // steps == iota(shape_left, 0) // SUB) & (item == my_tile)
        left_ref[pl.ds(chunk * item_height, item_height), :] = count_rows(left, right, True)
        shape_left = (tiles * SUB, LANES)
        left = (iota(shape_left, 1) // steps == me_tm - base) & (item == iota(shape_left, 0) // SUB)
        own_counts = own_counts + count_rows(left, right, False)
        column = chunk * LANES + iota((steps, LANES), 1)
        coeff = jnp.zeros((steps, LANES), F32)
        for shift, scale in ((-1, 1.0), (0, -2.0), (1, 1.0)):
            centre = coeff_rows + shift
            inside = (centre >= 1) & (centre <= total_steps - 2)
            apart = column - centre
            value = jnp.where(apart == 0, -2.0, jnp.where(jnp.abs(apart) == 1, 1.0, 0.0))
            coeff = coeff + jnp.where(inside, scale * value, 0.0)
        penalty = penalty + dot_nn(coeff.astype(BF16), dw.astype(BF16))
    left_ref[pl.ds(chunks * item_height, tiles * SUB), :] = jnp.concatenate([own_counts, own_counts], axis=1)

    per_tile = IT // rows

    def item_grams(m, carry):
        def gathered(first):
            return jnp.concatenate(
                [sent(m * per_tile + a, j, first, first + part) for a in range(per_tile) for j in range(peers)],
                axis=0,
            )

        v = gathered(0)
        gh_ref[m] = dot_tn(jnp.concatenate([v, gathered(part)], axis=1), v)
        return carry

    lax.fori_loop(0, tiles, item_grams, 0, unroll=tiles <= 2)

    sides = ([], [], [], [])
    for group in range(groups):
        sums = dot_nn(left_ref[...], gram_ref[group])
        s, d = sums[:, :R], sums[:, R:]
        at = pl.ds(group * SUB, SUB)
        below = pl.ds(R + group * SUB, SUB)
        a_rows = b_rows = q_rows = r_rows = jnp.zeros((SUB, R), F32)
        for a in range(tm):
            here = slice(a * SUB, (a + 1) * SUB)
            y, z = grams_ref[a, at, :], grams_ref[a, below, :]
            a_rows = a_rows + d[here] * y + s[here] * z
            b_rows = b_rows + s[here] * y
        for m in range(tiles):
            here = slice((tm + m) * SUB, (tm + m + 1) * SUB)
            g_m, h_m = gh_ref[m, at, :], gh_ref[m, below, :]
            q_rows = q_rows + d[here] * g_m + s[here] * h_m
            r_rows = r_rows + s[here] * g_m
        for side, value in zip(sides, (a_rows, b_rows, q_rows, r_rows)):
            side.append(value)
    left = jnp.concatenate([v_ref[...], dv_ref[...]], axis=1)
    item_rows = OBS_WEIGHT * dot_split(left, jnp.concatenate(sides[0] + sides[1], axis=0))
    left = jnp.concatenate([w_ref[...], dw_ref[...]], axis=1)
    time_rows = OBS_WEIGHT * dot_split(left, jnp.concatenate(sides[2] + sides[3], axis=0))
    first = jnp.where(me == 0, 1.0, 0.0)
    out_ref[:rows, :] = item_rows + (first * LAMBDA_ITEM) * dv_ref[...].astype(F32)
    out_ref[rows:, :] = time_rows + (first * LAMBDA_TIME) * penalty


def user_kernel(dims, u_hbm, du_hbm, wt_ref, ww_ref, gh_ref, entry_ref, out_hbm, u_ref, du_ref, out_ref, grams_ref, k_ref, in_sem, out_sem):
    tm, peers, tiles, steps, rows = dims
    chunks = wt_ref.shape[0]
    entries = LANES // steps
    blocks, groups = k_ref.shape[0], R // SUB
    loads = [
        pltpu.make_async_copy(u_hbm, u_ref, in_sem.at[0]),
        pltpu.make_async_copy(du_hbm, du_ref, in_sem.at[1]),
    ]
    for load in loads:
        load.start()

    width = LANES // (entries * SUB)

    def add(chunk, first, fresh):
        item, block = entry_ref[chunk, 0:1, :], entry_ref[chunk, 1:2, :]
        left = block == iota((blocks * SUB, LANES), 0) // SUB
        shape_right = (entries * width * SUB, LANES)
        place = iota(shape_right, 0) // SUB
        right = (iota(shape_right, 1) // steps == place // width) & (item == first + place % width)
        counts = count_rows(left, right, True)
        for group in range(groups):
            at = pl.ds(group * SUB, SUB)
            below = pl.ds(R + group * SUB, SUB)
            stack = []
            for a in range(entries):
                y, z = grams_ref[a, at, :], grams_ref[a, below, :]
                for m in range(width):
                    g_m, h_m = gh_ref[first + m, at, :], gh_ref[first + m, below, :]
                    stack.append(jnp.concatenate([g_m * y, g_m * z + h_m * y], axis=1))
            high, low = halves(jnp.concatenate(stack, axis=0))
            value = dot_nn(counts, jnp.concatenate([high, low], axis=0)).reshape(blocks, SUB, 2 * R)
            k_ref[:, at, :] = value if fresh else k_ref[:, at, :] + value

    for chunk in range(chunks):
        time_grams(wt_ref[chunk], ww_ref[chunk], grams_ref, 0, steps)
        add(chunk, 0, chunk == 0)

        def rest(i, carry):
            add(chunk, i * width, False)
            return carry

        lax.fori_loop(1, tiles // width, rest, 0)

    for load in loads:
        load.wait()
    stores = []
    per_store = blocks // out_sem.shape[0]
    for number in range(out_sem.shape[0]):
        for g in range(number * per_store, (number + 1) * per_store):
            at = pl.ds(g * UB, UB)
            du = du_ref[at, :]
            left = jnp.concatenate([du, u_ref[at, :]], axis=1)
            term = dot_split(left, jnp.concatenate([k_ref[g, :, :R], k_ref[g, :, R:]], axis=0))
            out_ref[at, :] = OBS_WEIGHT * term + LAMBDA_USER * du.astype(F32)
        at = pl.ds(number * per_store * UB, per_store * UB)
        store = pltpu.make_async_copy(out_ref.at[at, :], out_hbm.at[at, :], out_sem.at[number])
        store.start()
        stores.append(store)
    for store in stores:
        store.wait()


def finish_kernel(rows, *refs):
    item_ref, time_ref = refs[-2:]
    item_ref[...] = functools.reduce(jnp.add, [ref[:rows, :] for ref in refs[:-2]])
    time_ref[...] = functools.reduce(jnp.add, [ref[rows:, :] for ref in refs[:-2]])


def shape(dims, dtype=F32):
    return jax.ShapeDtypeStruct(dims, dtype)


def placed(small):
    if not small:
        return shape, lambda *arrays: arrays
    return pltpu.VMEM, lambda *arrays: [pltpu.with_memory_space_constraint(x, pltpu.VMEM) for x in arrays]


def body(user_factor, user_tangent, item_factor, item_tangent, time_factor, time_tangent, send_list, tile_slot, tile_item, tile_count):
    tm, peers = lax.axis_size("tm"), lax.axis_size("user")
    rows, steps = item_factor.shape[0], time_factor.shape[0]
    tiles = rows * tm // IT
    blocks = user_factor.shape[0] // UB
    dims = (tm, peers, tiles, steps, rows)
    chunks = tm * steps // LANES
    near, held = placed(chunks == 1 and tiles <= 2)
    height = 2 * rows // peers + 2 * steps // peers + 8
    packed = pl.pallas_call(
        functools.partial(pack_kernel, dims),
        out_shape=shape((tm * peers // 2, height, R), BF16),
        in_specs=[VM] * 4 + [SM] * 4,
        out_specs=VM,
        scratch_shapes=[pltpu.VMEM((2 * steps, R), F32)],
        name="pack",
    )(item_factor, item_tangent, time_factor, time_tangent, send_list, tile_slot, tile_item, tile_count)
    groups = R // SUB
    grams = pl.pallas_call(
        gram_kernel,
        out_shape=near((groups, 2 * SUB * blocks, 2 * R), BF16),
        in_specs=[VM] * 2,
        out_specs=VM,
        name="grams",
    )(user_factor, user_tangent)
    cores = [[i for i in range(tm * peers) if i % 2 == core] for core in range(2)]
    got = lax.all_to_all(
        packed, ("tm", "user"), split_axis=0, concat_axis=0, tiled=True, axis_index_groups=cores
    )
    got, grams = lax.optimization_barrier((got, grams))
    other = lax.ppermute(got, "user", [(i, i ^ 1) for i in range(peers)])
    partial, wt, ww, gh, listed = pl.pallas_call(
        functools.partial(partial_kernel, dims),
        out_shape=(
            near((rows + steps, R), F32),
            near((chunks, 2 * R, LANES), BF16),
            near((chunks, LANES, R), BF16),
            near((tiles, 2 * R, R), F32),
            near((chunks, 8, LANES), jnp.int32),
        ),
        in_specs=[VM] * 7,
        out_specs=(VM,) * 5,
        scratch_shapes=[
            pltpu.VMEM(((tm + tiles) * SUB, 2 * SUB * blocks), BF16),
            pltpu.VMEM((tm, 2 * R, R), F32),
        ],
        name="partials",
    )(*held(got, other, grams), item_factor, item_tangent, time_factor, time_tangent)
    others = [lax.ppermute(partial, "user", [(i, i ^ d) for i in range(peers)]) for d in range(1, peers)]
    user_hvp = pl.pallas_call(
        functools.partial(user_kernel, dims),
        out_shape=shape(user_factor.shape),
        in_specs=[HBM] * 2 + [VM] * 4,
        out_specs=HBM,
        scratch_shapes=[
            pltpu.VMEM(user_factor.shape, BF16),
            pltpu.VMEM(user_factor.shape, BF16),
            pltpu.VMEM(user_factor.shape, F32),
            pltpu.VMEM((LANES // steps, 2 * R, R), F32),
            pltpu.VMEM((blocks, R, 2 * R), F32),
            pltpu.SemaphoreType.DMA((2,)),
            pltpu.SemaphoreType.DMA((4,)),
        ],
        name="user_rows",
    )(user_factor, user_tangent, *held(wt, ww, gh, listed))
    item_hvp, time_hvp = pl.pallas_call(
        functools.partial(finish_kernel, rows),
        out_shape=(shape((rows, R)), shape((steps, R))),
        in_specs=[VM] * peers,
        out_specs=(VM, VM),
        name="finish",
    )(*held(partial), *held(*others))
    return (user_hvp, item_hvp, time_hvp)


def solution(mesh):
    return jax.shard_map(
        body,
        mesh=mesh,
        in_specs=(
            P("user", None),
            P("user", None),
            P("tm", None),
            P("tm", None),
            P("tm", None),
            P("tm", None),
            P("tm", "user", None, None),
            P("tm", "user", None),
            P("tm", "user", None),
            P("tm", "user"),
        ),
        out_specs=(P("user", None), P("tm", None), P("tm", None)),
        check_vma=False,
    )
```

```python
import functools

import jax
import jax.numpy as jnp
from jax import lax
from jax.experimental import pallas as pl
from jax.experimental.pallas import tpu as pltpu
from jax.sharding import PartitionSpec as P

R = 128
UB = 128
IT = 256
LANES = 128
SUB = 8

OBS_WEIGHT = 0.03125
LAMBDA_USER = 0.5
LAMBDA_ITEM = 0.5
LAMBDA_TIME = 1.0

F32 = jnp.float32
BF16 = jnp.bfloat16
VM = pl.BlockSpec(memory_space=pltpu.VMEM)
HBM = pl.BlockSpec(memory_space=pltpu.HBM)
SM = pl.BlockSpec(memory_space=pltpu.SMEM)


def iota(shape, dim):
    return lax.broadcasted_iota(jnp.int32, shape, dim)


def dot_tn(left, right):
    return lax.dot_general(left, right, (((0,), (0,)), ((), ())), preferred_element_type=F32)


def dot_nn(left, right):
    return lax.dot_general(left, right, (((1,), (0,)), ((), ())), preferred_element_type=F32)


def halves(values):
    high = values.astype(BF16)
    return high, (values - high.astype(F32)).astype(BF16)


def dot_split(left, right):
    both = dot_nn(left, jnp.concatenate(halves(right), axis=1))
    width = right.shape[1]
    return both[:, :width] + both[:, width:]


def pack_kernel(dims, v_ref, dv_ref, w_ref, dw_ref, send_ref, slot_ref, item_ref, count_ref, out_ref, time_ref):
    tm, peers, tiles, steps, rows = dims
    me = lax.axis_index("user")
    part = rows // peers
    start = pl.multiple_of(me * part, part)
    time_ref[0:steps, :] = w_ref[...].astype(F32)
    time_ref[steps:, :] = dw_ref[...].astype(F32)
    piece = 2 * steps // peers
    time_rows = time_ref[pl.ds(pl.multiple_of(me * piece, piece), piece), :]
    slots = send_ref.shape[3]
    row, lane = iota((8, LANES), 0), iota((8, LANES), 1)
    wanted = row * slots + lane % slots
    table = jnp.full((8, LANES), -1, jnp.int32)
    count = count_ref[0, 0]
    for n in range(slot_ref.shape[2]):
        hit = (wanted == slot_ref[0, 0, n]) & (n < count)
        table = jnp.where(hit, item_ref[0, 0, n], table)
    entry = lane % (peers * slots)
    for j in range(peers):
        for s in range(slots):
            table = jnp.where((row == peers) & (entry == j * slots + s), send_ref[0, 0, j, s], table)
    last = jnp.concatenate([time_rows, table.astype(F32)], axis=0).astype(BF16)
    whole = jnp.concatenate([v_ref[pl.ds(start, part), :], dv_ref[pl.ds(start, part), :], last], axis=0)
    out_ref[...] = jnp.broadcast_to(whole[None], out_ref.shape)


def gram_kernel(u_ref, du_ref, out_ref):
    blocks = u_ref.shape[0] // UB
    groups = R // SUB

    def pair(i, carry):
        sides = []
        for g in (2 * i, 2 * i + 1):
            at = pl.ds(pl.multiple_of(g * UB, UB), UB)
            u = u_ref[at, :]
            gram = dot_tn(jnp.concatenate([u, du_ref[at, :]], axis=1), u)
            sides.append(jnp.concatenate([gram[:R], gram[R:]], axis=1).reshape(groups, SUB, 2 * R))
        high, low = halves(jnp.concatenate(sides, axis=1))
        at = pl.multiple_of(i * 2 * SUB, 2 * SUB)
        out_ref[:, pl.ds(at, 2 * SUB), :] = high
        out_ref[:, pl.ds(at + blocks * SUB, 2 * SUB), :] = low
        return carry

    lax.fori_loop(0, blocks // 2, pair, 0, unroll=2)


def dot_nt(left, right):
    return lax.dot_general(left, right, (((1,), (1,)), ((), ())), preferred_element_type=F32)


def count_rows(left, right, keep):
    counts = dot_nt(left.astype(BF16), right.astype(BF16))
    same = iota(counts.shape, 0) % SUB == iota(counts.shape, 1) % SUB
    counts = jnp.where(same, counts, 0.0).astype(BF16)
    return jnp.concatenate([counts, counts], axis=1) if keep else counts


def time_grams(wt, w, out_ref, at, steps):
    owner = iota((LANES, R), 0) // steps
    zero = jnp.zeros((LANES, R), BF16)
    for a in range(0, LANES // steps, 2):
        right = jnp.concatenate([jnp.where(owner == a + i, w, zero) for i in range(2)], axis=1)
        both = dot_nn(wt, right)
        out_ref[at + a] = both[:, :R]
        out_ref[at + a + 1] = both[:, R:]


def partial_kernel(dims, got_ref, other_ref, gram_ref, out_ref, wt_ref, ww_ref, gh_ref, entry_ref, left_ref, grams_ref):
    tm, peers, tiles, steps, rows = dims
    groups, depth = gram_ref.shape[:2]
    blocks = depth // (2 * SUB)
    part = rows // peers
    piece = 2 * steps // peers
    entries = LANES // steps
    chunks = tm // entries
    me_tm, me = lax.axis_index("tm"), lax.axis_index("user")
    lane, row8 = iota((8, LANES), 1), iota((8, LANES), 0)
    slots = steps // peers

    def sent(a, j, first, last):
        here = a * (peers // 2) + j // 2
        return jnp.where(me % 2 == j % 2, got_ref[here, first:last, :], other_ref[here, first:last, :])

    my_tile = me_tm * rows // IT

    coeff_rows = me_tm * steps + iota((steps, LANES), 0)
    penalty = jnp.zeros((steps, R), F32)
    total_steps = tm * steps
    item_height = entries * SUB
    own_counts = jnp.zeros((tiles * SUB, blocks * SUB), BF16)
    for chunk in range(chunks):
        base = chunk * entries
        pieces = []
        found_m = jnp.zeros((8, LANES), F32)
        found_g = jnp.zeros((8, LANES), F32)
        for a in range(entries):
            for j in range(peers):
                tile = sent(base + a, j, 2 * part, 2 * part + 16).astype(F32)
                pieces.append(tile[:piece])
                mine = lane // steps == a
                hit = mine & (row8 == me) & (lane // slots % peers == j)
                found_m = found_m + jnp.where(hit, tile[piece:], 0.0)
                hit = mine & (row8 == peers) & (me == j)
                found_g = found_g + jnp.where(hit, tile[piece:], 0.0)
        half = peers // 2
        w = jnp.concatenate([pieces[a * peers + j] for a in range(entries) for j in range(half)], axis=0)
        dw = jnp.concatenate([pieces[a * peers + j] for a in range(entries) for j in range(half, peers)], axis=0)
        wt_ref[chunk] = jnp.concatenate([w, dw], axis=1).T.astype(BF16)
        ww_ref[chunk] = w.astype(BF16)
        time_grams(wt_ref[chunk], ww_ref[chunk], grams_ref, base, steps)
        item = jnp.sum(found_m, axis=0, keepdims=True).astype(jnp.int32)
        block = jnp.sum(found_g, axis=0, keepdims=True).astype(jnp.int32)
        entry_ref[chunk, 0:1, :] = item
        entry_ref[chunk, 1:2, :] = block
        shape_left, shape_right = (item_height, LANES), (blocks * SUB, LANES)
        right = block == iota(shape_right, 0) // SUB
        left = (iota(shape_left, 1) // steps == iota(shape_left, 0) // SUB) & (item == my_tile)
        left_ref[pl.ds(chunk * item_height, item_height), :] = count_rows(left, right, True)
        shape_left = (tiles * SUB, LANES)
        left = (iota(shape_left, 1) // steps == me_tm - base) & (item == iota(shape_left, 0) // SUB)
        own_counts = own_counts + count_rows(left, right, False)
        column = chunk * LANES + iota((steps, LANES), 1)
        coeff = jnp.zeros((steps, LANES), F32)
        for shift, scale in ((-1, 1.0), (0, -2.0), (1, 1.0)):
            centre = coeff_rows + shift
            inside = (centre >= 1) & (centre <= total_steps - 2)
            apart = column - centre
            value = jnp.where(apart == 0, -2.0, jnp.where(jnp.abs(apart) == 1, 1.0, 0.0))
            coeff = coeff + jnp.where(inside, scale * value, 0.0)
        penalty = penalty + dot_nn(coeff.astype(BF16), dw.astype(BF16))
    left_ref[pl.ds(chunks * item_height, tiles * SUB), :] = jnp.concatenate([own_counts, own_counts], axis=1)

    per_tile = IT // rows

    def item_grams(m, carry):
        def gathered(first):
            return jnp.concatenate(
                [sent(m * per_tile + a, j, first, first + part) for a in range(per_tile) for j in range(peers)],
                axis=0,
            )

        v = gathered(0)
        gh_ref[m] = OBS_WEIGHT * dot_tn(jnp.concatenate([v, gathered(part)], axis=1), v)
        return carry

    lax.fori_loop(0, tiles, item_grams, 0, unroll=tiles <= 2)

    sides = ([], [], [], [])
    for group in range(groups):
        sums = dot_nn(left_ref[...], gram_ref[group])
        s, d = sums[:, :R], sums[:, R:]
        at = pl.ds(group * SUB, SUB)
        below = pl.ds(R + group * SUB, SUB)
        a_rows = b_rows = q_rows = r_rows = jnp.zeros((SUB, R), F32)
        for a in range(tm):
            here = slice(a * SUB, (a + 1) * SUB)
            y, z = grams_ref[a, at, :], grams_ref[a, below, :]
            a_rows = a_rows + d[here] * y + s[here] * z
            b_rows = b_rows + s[here] * y
        for m in range(tiles):
            here = slice((tm + m) * SUB, (tm + m + 1) * SUB)
            g_m, h_m = gh_ref[m, at, :], gh_ref[m, below, :]
            q_rows = q_rows + d[here] * g_m + s[here] * h_m
            r_rows = r_rows + s[here] * g_m
        for side, value in zip(sides, (a_rows, b_rows, q_rows, r_rows)):
            side.append(value)
    v_own = jnp.concatenate([sent(me_tm, j, 0, part) for j in range(peers)], axis=0)
    dv_own = jnp.concatenate([sent(me_tm, j, part, 2 * part) for j in range(peers)], axis=0)
    left = jnp.concatenate([v_own, dv_own], axis=1)
    item_rows = OBS_WEIGHT * dot_split(left, jnp.concatenate(sides[0] + sides[1], axis=0))
    own = [sent(me_tm, j, 2 * part, 2 * part + 16).astype(F32)[:piece] for j in range(peers)]
    left = jnp.concatenate([jnp.concatenate(own[:half], axis=0), jnp.concatenate(own[half:], axis=0)], axis=1)
    time_rows = dot_split(left.astype(BF16), jnp.concatenate(sides[2] + sides[3], axis=0))
    first = jnp.where(me == 0, 1.0, 0.0)
    out_ref[:rows, :] = item_rows + (first * LAMBDA_ITEM) * dv_own.astype(F32)
    out_ref[rows:, :] = time_rows + (first * LAMBDA_TIME) * penalty


def user_kernel(dims, u_hbm, du_hbm, wt_ref, ww_ref, gh_ref, entry_ref, out_hbm, u_ref, du_ref, out_ref, grams_ref, k_ref, in_sem, out_sem):
    tm, peers, tiles, steps, rows = dims
    chunks = wt_ref.shape[0]
    entries = LANES // steps
    blocks, groups = k_ref.shape[0], R // SUB
    loads = [
        pltpu.make_async_copy(u_hbm, u_ref, in_sem.at[0]),
        pltpu.make_async_copy(du_hbm, du_ref, in_sem.at[1]),
    ]
    for load in loads:
        load.start()

    width = LANES // (entries * SUB)

    def add(chunk, first, fresh):
        item, block = entry_ref[chunk, 0:1, :], entry_ref[chunk, 1:2, :]
        left = block == iota((blocks * SUB, LANES), 0) // SUB
        shape_right = (entries * width * SUB, LANES)
        place = iota(shape_right, 0) // SUB
        right = (iota(shape_right, 1) // steps == place // width) & (item == first + place % width)
        counts = count_rows(left, right, True)
        def rows_of(group, carry):
            at = pl.ds(pl.multiple_of(group * SUB, SUB), SUB)
            below = pl.ds(pl.multiple_of(R + group * SUB, SUB), SUB)
            stack = []
            for a in range(entries):
                y, z = grams_ref[a, at, :], grams_ref[a, below, :]
                for m in range(width):
                    g_m, h_m = gh_ref[first + m, at, :], gh_ref[first + m, below, :]
                    stack.append(jnp.concatenate([g_m * y, g_m * z + h_m * y], axis=1))
            high, low = halves(jnp.concatenate(stack, axis=0))
            value = dot_nn(counts, jnp.concatenate([high, low], axis=0)).reshape(blocks, SUB, 2 * R)
            if fresh:
                eye = iota((SUB, 2 * R), 0) + group * SUB == iota((SUB, 2 * R), 1)
                value = value + jnp.where(eye, LAMBDA_USER, 0.0)[None]
            k_ref[:, at, :] = value if fresh else k_ref[:, at, :] + value
            return carry

        lax.fori_loop(0, groups, rows_of, 0, unroll=8)

    for chunk in range(chunks):
        time_grams(wt_ref[chunk], ww_ref[chunk], grams_ref, 0, steps)
        add(chunk, 0, chunk == 0)

        def rest(i, carry):
            add(chunk, i * width, False)
            return carry

        lax.fori_loop(1, tiles // width, rest, 0)

    for load in loads:
        load.wait()
    stores = []
    per_store = blocks // out_sem.shape[0]
    for number in range(out_sem.shape[0]):
        for g in range(number * per_store, (number + 1) * per_store):
            at = pl.ds(g * UB, UB)
            left = jnp.concatenate([du_ref[at, :], u_ref[at, :]], axis=1)
            out_ref[at, :] = dot_split(left, jnp.concatenate([k_ref[g, :, :R], k_ref[g, :, R:]], axis=0))
        at = pl.ds(number * per_store * UB, per_store * UB)
        store = pltpu.make_async_copy(out_ref.at[at, :], out_hbm.at[at, :], out_sem.at[number])
        store.start()
        stores.append(store)
    for store in stores:
        store.wait()


def finish_kernel(rows, *refs):
    item_ref, time_ref = refs[-2:]
    item_ref[...] = functools.reduce(jnp.add, [ref[:rows, :] for ref in refs[:-2]])
    time_ref[...] = functools.reduce(jnp.add, [ref[rows:, :] for ref in refs[:-2]])


def shape(dims, dtype=F32):
    return jax.ShapeDtypeStruct(dims, dtype)


def placed(small):
    if not small:
        return shape, lambda *arrays: arrays
    return pltpu.VMEM, lambda *arrays: [pltpu.with_memory_space_constraint(x, pltpu.VMEM) for x in arrays]


def body(user_factor, user_tangent, item_factor, item_tangent, time_factor, time_tangent, send_list, tile_slot, tile_item, tile_count):
    tm, peers = lax.axis_size("tm"), lax.axis_size("user")
    rows, steps = item_factor.shape[0], time_factor.shape[0]
    tiles = rows * tm // IT
    blocks = user_factor.shape[0] // UB
    dims = (tm, peers, tiles, steps, rows)
    chunks = tm * steps // LANES
    near, held = placed(chunks == 1 and tiles <= 2)
    height = 2 * rows // peers + 2 * steps // peers + 8
    packed = pl.pallas_call(
        functools.partial(pack_kernel, dims),
        out_shape=shape((tm * peers // 2, height, R), BF16),
        in_specs=[VM] * 4 + [SM] * 4,
        out_specs=VM,
        scratch_shapes=[pltpu.VMEM((2 * steps, R), F32)],
        name="pack",
    )(item_factor, item_tangent, time_factor, time_tangent, send_list, tile_slot, tile_item, tile_count)
    groups = R // SUB
    grams = pl.pallas_call(
        gram_kernel,
        out_shape=near((groups, 2 * SUB * blocks, 2 * R), BF16),
        in_specs=[VM] * 2,
        out_specs=VM,
        name="grams",
    )(user_factor, user_tangent)
    cores = [[i for i in range(tm * peers) if i % 2 == core] for core in range(2)]
    got = lax.all_to_all(
        packed, ("tm", "user"), split_axis=0, concat_axis=0, tiled=True, axis_index_groups=cores
    )
    got, grams = lax.optimization_barrier((got, grams))
    other = lax.ppermute(got, "user", [(i, i ^ 1) for i in range(peers)])
    partial, wt, ww, gh, listed = pl.pallas_call(
        functools.partial(partial_kernel, dims),
        out_shape=(
            near((rows + steps, R), F32),
            near((chunks, 2 * R, LANES), BF16),
            near((chunks, LANES, R), BF16),
            near((tiles, 2 * R, R), F32),
            near((chunks, 8, LANES), jnp.int32),
        ),
        in_specs=[VM] * 3,
        out_specs=(VM,) * 5,
        scratch_shapes=[
            pltpu.VMEM(((tm + tiles) * SUB, 2 * SUB * blocks), BF16),
            pltpu.VMEM((tm, 2 * R, R), F32),
        ],
        name="partials",
    )(*held(got, other, grams))
    others = [lax.ppermute(partial, "user", [(i, i ^ d) for i in range(peers)]) for d in range(1, peers)]
    user_hvp = pl.pallas_call(
        functools.partial(user_kernel, dims),
        out_shape=shape(user_factor.shape),
        in_specs=[HBM] * 2 + [VM] * 4,
        out_specs=HBM,
        scratch_shapes=[
            pltpu.VMEM(user_factor.shape, BF16),
            pltpu.VMEM(user_factor.shape, BF16),
            pltpu.VMEM(user_factor.shape, F32),
            pltpu.VMEM((LANES // steps, 2 * R, R), F32),
            pltpu.VMEM((blocks, R, 2 * R), F32),
            pltpu.SemaphoreType.DMA((2,)),
            pltpu.SemaphoreType.DMA((4,)),
        ],
        name="user_rows",
    )(user_factor, user_tangent, *held(wt, ww, gh, listed))
    item_hvp, time_hvp = pl.pallas_call(
        functools.partial(finish_kernel, rows),
        out_shape=(shape((rows, R)), shape((steps, R))),
        in_specs=[VM] * peers,
        out_specs=(VM, VM),
        name="finish",
    )(*held(partial), *held(*others))
    return (user_hvp, item_hvp, time_hvp)


def solution(mesh):
    return jax.shard_map(
        body,
        mesh=mesh,
        in_specs=(
            P("user", None),
            P("user", None),
            P("tm", None),
            P("tm", None),
            P("tm", None),
            P("tm", None),
            P("tm", "user", None, None),
            P("tm", "user", None),
            P("tm", "user", None),
            P("tm", "user"),
        ),
        out_specs=(P("user", None), P("tm", None), P("tm", None)),
        check_vma=False,
    )
```

```python
import functools

import jax
import jax.numpy as jnp
from jax import lax
from jax.experimental import pallas as pl
from jax.experimental.pallas import tpu as pltpu
from jax.sharding import PartitionSpec as P

R = 128
UB = 128
IT = 256
LANES = 128
SUB = 8

OBS_WEIGHT = 0.03125
LAMBDA_USER = 0.5
LAMBDA_ITEM = 0.5
LAMBDA_TIME = 1.0

F32 = jnp.float32
BF16 = jnp.bfloat16
VM = pl.BlockSpec(memory_space=pltpu.VMEM)
HBM = pl.BlockSpec(memory_space=pltpu.HBM)
SM = pl.BlockSpec(memory_space=pltpu.SMEM)


def iota(shape, dim):
    return lax.broadcasted_iota(jnp.int32, shape, dim)


def dot_tn(left, right):
    return lax.dot_general(left, right, (((0,), (0,)), ((), ())), preferred_element_type=F32)


def dot_nn(left, right):
    return lax.dot_general(left, right, (((1,), (0,)), ((), ())), preferred_element_type=F32)


def halves(values):
    high = values.astype(BF16)
    return high, (values - high.astype(F32)).astype(BF16)


def dot_split(left, right):
    both = dot_nn(left, jnp.concatenate(halves(right), axis=1))
    width = right.shape[1]
    return both[:, :width] + both[:, width:]


def pack_kernel(dims, v_ref, dv_ref, w_ref, dw_ref, send_ref, slot_ref, item_ref, count_ref, out_ref, time_ref):
    tm, peers, tiles, steps, rows = dims
    me = lax.axis_index("user")
    part = rows // peers
    start = pl.multiple_of(me * part, part)
    time_ref[0, :, :] = w_ref[...].astype(F32)
    time_ref[1, :, :] = dw_ref[...].astype(F32)
    slots = send_ref.shape[3]
    row, lane = iota((SUB, LANES), 0), iota((SUB, LANES), 1)
    sent_list = jnp.zeros((SUB, LANES), jnp.int32)
    entry = lane % (peers * slots)
    for j in range(peers):
        for s in range(slots):
            sent_list = jnp.where(entry == j * slots + s, send_ref[0, 0, j, s], sent_list)
    count = count_ref[0, 0]
    at = pl.multiple_of(me // 2 * SUB, SUB)
    for k in range(peers):
        table = jnp.full((SUB, LANES), -1, jnp.int32)
        for n in range(slot_ref.shape[2]):
            hit = (lane % slots + k * slots == slot_ref[0, 0, n]) & (n < count)
            table = jnp.where(hit, item_ref[0, 0, n], table)
        lists = jnp.where(row % 4 == 0, table, sent_list).astype(F32)
        last = jnp.where(row // 4 == me % 2, time_ref[k % 2, pl.ds(at, SUB), :], lists).astype(BF16)
        first = (dv_ref if k % 2 else v_ref)[pl.ds(start, part), :]
        out_ref[:, k, :part, :] = jnp.broadcast_to(first[None], (tm, part, R))
        out_ref[:, k, part:, :] = jnp.broadcast_to(last[None], (tm, SUB, R))


def gram_kernel(u_ref, du_ref, out_ref):
    blocks = u_ref.shape[0] // UB
    groups = R // SUB

    def pair(i, carry):
        sides = []
        for g in (2 * i, 2 * i + 1):
            at = pl.ds(pl.multiple_of(g * UB, UB), UB)
            u = u_ref[at, :]
            gram = dot_tn(jnp.concatenate([u, du_ref[at, :]], axis=1), u)
            sides.append(jnp.concatenate([gram[:R], gram[R:]], axis=1).reshape(groups, SUB, 2 * R))
        high, low = halves(jnp.concatenate(sides, axis=1))
        at = pl.multiple_of(i * 2 * SUB, 2 * SUB)
        out_ref[:, pl.ds(at, 2 * SUB), :] = high
        out_ref[:, pl.ds(at + blocks * SUB, 2 * SUB), :] = low
        return carry

    lax.fori_loop(0, blocks // 2, pair, 0, unroll=2)


def dot_nt(left, right):
    return lax.dot_general(left, right, (((1,), (1,)), ((), ())), preferred_element_type=F32)


def count_rows(left, right, keep):
    counts = dot_nt(left.astype(BF16), right.astype(BF16))
    same = iota(counts.shape, 0) % SUB == iota(counts.shape, 1) % SUB
    counts = jnp.where(same, counts, 0.0).astype(BF16)
    return jnp.concatenate([counts, counts], axis=1) if keep else counts


def time_grams(wt, w, out_ref, at, steps):
    owner = iota((LANES, R), 0) // steps
    zero = jnp.zeros((LANES, R), BF16)
    for a in range(0, LANES // steps, 2):
        right = jnp.concatenate([jnp.where(owner == a + i, w, zero) for i in range(2)], axis=1)
        both = dot_nn(wt, right)
        out_ref[at + a] = both[:, :R]
        out_ref[at + a + 1] = both[:, R:]


def partial_kernel(dims, got_ref, other_ref, gram_ref, out_ref, wt_ref, ww_ref, gh_ref, entry_ref, left_ref, grams_ref):
    tm, peers, tiles, steps, rows = dims
    groups, depth = gram_ref.shape[:2]
    blocks = depth // (2 * SUB)
    part = rows // peers
    entries = LANES // steps
    chunks = tm // entries
    me_tm, me = lax.axis_index("tm"), lax.axis_index("user")
    lane, row8 = iota((8, LANES), 1), iota((8, LANES), 0)
    slots = steps // peers
    even = me % 2 == 0

    def sent(a, j, kind):
        here = a * peers + j
        return jnp.where(even == (kind == 0), got_ref[here, :part, :], other_ref[here, :part, :])

    def time_rows_of(a):
        lasts = [[ref[a * peers + j, part:, :].astype(F32) for j in range(peers)] for ref in (got_ref, other_ref)]
        sides = []
        for kind in range(2):
            pieces = [jnp.where(even == (kind == 0), lasts[0][j], lasts[1][j]) for j in range(peers)]
            sides.append(jnp.concatenate([jnp.where(row8 < 4, *pieces[j : j + 2]) for j in range(0, peers, 2)], axis=0))
        return sides, lasts[0]

    my_tile = me_tm * rows // IT

    coeff_rows = me_tm * steps + iota((steps, LANES), 0)
    penalty = jnp.zeros((steps, R), F32)
    total_steps = tm * steps
    item_height = entries * SUB
    own_counts = jnp.zeros((tiles * SUB, blocks * SUB), BF16)
    for chunk in range(chunks):
        base = chunk * entries
        found_m = jnp.zeros((8, LANES), F32)
        found_g = jnp.zeros((8, LANES), F32)
        sides = ([], [])
        for a in range(entries):
            both, lasts = time_rows_of(base + a)
            sides[0].append(both[0])
            sides[1].append(both[1])
            mine = lane // steps == a
            for j in range(peers):
                at = 0 if j % 2 else 4
                hit = mine & (row8 == at) & (lane // slots % peers == j)
                found_m = found_m + jnp.where(hit, lasts[j], 0.0)
                hit = mine & (row8 == at + 1) & (me == j)
                found_g = found_g + jnp.where(hit, lasts[j], 0.0)
        w, dw = jnp.concatenate(sides[0], axis=0), jnp.concatenate(sides[1], axis=0)
        wt_ref[chunk] = jnp.concatenate([w, dw], axis=1).T.astype(BF16)
        ww_ref[chunk] = w.astype(BF16)
        time_grams(wt_ref[chunk], ww_ref[chunk], grams_ref, base, steps)
        item = jnp.sum(found_m, axis=0, keepdims=True).astype(jnp.int32)
        block = jnp.sum(found_g, axis=0, keepdims=True).astype(jnp.int32)
        entry_ref[chunk, 0:1, :] = item
        entry_ref[chunk, 1:2, :] = block
        shape_left, shape_right = (item_height, LANES), (blocks * SUB, LANES)
        right = block == iota(shape_right, 0) // SUB
        left = (iota(shape_left, 1) // steps == iota(shape_left, 0) // SUB) & (item == my_tile)
        left_ref[pl.ds(chunk * item_height, item_height), :] = count_rows(left, right, True)
        shape_left = (tiles * SUB, LANES)
        left = (iota(shape_left, 1) // steps == me_tm - base) & (item == iota(shape_left, 0) // SUB)
        own_counts = own_counts + count_rows(left, right, False)
        column = chunk * LANES + iota((steps, LANES), 1)
        coeff = jnp.zeros((steps, LANES), F32)
        for shift, scale in ((-1, 1.0), (0, -2.0), (1, 1.0)):
            centre = coeff_rows + shift
            inside = (centre >= 1) & (centre <= total_steps - 2)
            apart = column - centre
            value = jnp.where(apart == 0, -2.0, jnp.where(jnp.abs(apart) == 1, 1.0, 0.0))
            coeff = coeff + jnp.where(inside, scale * value, 0.0)
        penalty = penalty + dot_nn(coeff.astype(BF16), dw.astype(BF16))
    left_ref[pl.ds(chunks * item_height, tiles * SUB), :] = jnp.concatenate([own_counts, own_counts], axis=1)

    per_tile = IT // rows

    def item_grams(m, carry):
        def gathered(kind):
            return jnp.concatenate([sent(m * per_tile + a, j, kind) for a in range(per_tile) for j in range(peers)], axis=0)

        v = gathered(0)
        gh_ref[m] = OBS_WEIGHT * dot_tn(jnp.concatenate([v, gathered(1)], axis=1), v)
        return carry

    lax.fori_loop(0, tiles, item_grams, 0, unroll=tiles <= 2)

    sides = ([], [], [], [])
    for group in range(groups):
        sums = dot_nn(left_ref[...], gram_ref[group])
        s, d = sums[:, :R], sums[:, R:]
        at = pl.ds(group * SUB, SUB)
        below = pl.ds(R + group * SUB, SUB)
        a_rows = b_rows = q_rows = r_rows = jnp.zeros((SUB, R), F32)
        for a in range(tm):
            here = slice(a * SUB, (a + 1) * SUB)
            y, z = grams_ref[a, at, :], grams_ref[a, below, :]
            a_rows = a_rows + d[here] * y + s[here] * z
            b_rows = b_rows + s[here] * y
        for m in range(tiles):
            here = slice((tm + m) * SUB, (tm + m + 1) * SUB)
            g_m, h_m = gh_ref[m, at, :], gh_ref[m, below, :]
            q_rows = q_rows + d[here] * g_m + s[here] * h_m
            r_rows = r_rows + s[here] * g_m
        for side, value in zip(sides, (a_rows, b_rows, q_rows, r_rows)):
            side.append(value)
    v_own = jnp.concatenate([sent(me_tm, j, 0) for j in range(peers)], axis=0)
    dv_own = jnp.concatenate([sent(me_tm, j, 1) for j in range(peers)], axis=0)
    left = jnp.concatenate([v_own, dv_own], axis=1)
    item_rows = OBS_WEIGHT * dot_split(left, jnp.concatenate(sides[0] + sides[1], axis=0))
    left = jnp.concatenate(time_rows_of(me_tm)[0], axis=1)
    time_rows = dot_split(left.astype(BF16), jnp.concatenate(sides[2] + sides[3], axis=0))
    first = jnp.where(me == 0, 1.0, 0.0)
    out_ref[:rows, :] = item_rows + (first * LAMBDA_ITEM) * dv_own.astype(F32)
    out_ref[rows:, :] = time_rows + (first * LAMBDA_TIME) * penalty


def user_kernel(dims, u_hbm, du_hbm, wt_ref, ww_ref, gh_ref, entry_ref, out_hbm, u_ref, du_ref, out_ref, grams_ref, k_ref, in_sem, out_sem):
    tm, peers, tiles, steps, rows = dims
    chunks = wt_ref.shape[0]
    entries = LANES // steps
    blocks, groups = k_ref.shape[0], R // SUB
    loads = [
        pltpu.make_async_copy(u_hbm, u_ref, in_sem.at[0]),
        pltpu.make_async_copy(du_hbm, du_ref, in_sem.at[1]),
    ]
    for load in loads:
        load.start()

    width = LANES // (entries * SUB)

    def add(chunk, first, fresh):
        item, block = entry_ref[chunk, 0:1, :], entry_ref[chunk, 1:2, :]
        left = block == iota((blocks * SUB, LANES), 0) // SUB
        shape_right = (entries * width * SUB, LANES)
        place = iota(shape_right, 0) // SUB
        right = (iota(shape_right, 1) // steps == place // width) & (item == first + place % width)
        counts = count_rows(left, right, True)
        def rows_of(group, carry):
            at = pl.ds(pl.multiple_of(group * SUB, SUB), SUB)
            below = pl.ds(pl.multiple_of(R + group * SUB, SUB), SUB)
            stack = []
            for a in range(entries):
                y, z = grams_ref[a, at, :], grams_ref[a, below, :]
                for m in range(width):
                    g_m, h_m = gh_ref[first + m, at, :], gh_ref[first + m, below, :]
                    stack.append(jnp.concatenate([g_m * y, g_m * z + h_m * y], axis=1))
            high, low = halves(jnp.concatenate(stack, axis=0))
            value = dot_nn(counts, jnp.concatenate([high, low], axis=0)).reshape(blocks, SUB, 2 * R)
            if fresh:
                eye = iota((SUB, 2 * R), 0) + group * SUB == iota((SUB, 2 * R), 1)
                value = value + jnp.where(eye, LAMBDA_USER, 0.0)[None]
            k_ref[:, at, :] = value if fresh else k_ref[:, at, :] + value
            return carry

        lax.fori_loop(0, groups, rows_of, 0, unroll=8)

    for chunk in range(chunks):
        time_grams(wt_ref[chunk], ww_ref[chunk], grams_ref, 0, steps)
        add(chunk, 0, chunk == 0)

        def rest(i, carry):
            add(chunk, i * width, False)
            return carry

        lax.fori_loop(1, tiles // width, rest, 0)

    for load in loads:
        load.wait()
    stores = []
    per_store = blocks // out_sem.shape[0]
    for number in range(out_sem.shape[0]):
        for g in range(number * per_store, (number + 1) * per_store):
            at = pl.ds(g * UB, UB)
            left = jnp.concatenate([du_ref[at, :], u_ref[at, :]], axis=1)
            out_ref[at, :] = dot_split(left, jnp.concatenate([k_ref[g, :, :R], k_ref[g, :, R:]], axis=0))
        at = pl.ds(number * per_store * UB, per_store * UB)
        store = pltpu.make_async_copy(out_ref.at[at, :], out_hbm.at[at, :], out_sem.at[number])
        store.start()
        stores.append(store)
    for store in stores:
        store.wait()


def finish_kernel(rows, *refs):
    item_ref, time_ref = refs[-2:]
    item_ref[...] = functools.reduce(jnp.add, [ref[:rows, :] for ref in refs[:-2]])
    time_ref[...] = functools.reduce(jnp.add, [ref[rows:, :] for ref in refs[:-2]])


def shape(dims, dtype=F32):
    return jax.ShapeDtypeStruct(dims, dtype)


def placed(small):
    if not small:
        return shape, lambda *arrays: arrays
    return pltpu.VMEM, lambda *arrays: [pltpu.with_memory_space_constraint(x, pltpu.VMEM) for x in arrays]


def body(user_factor, user_tangent, item_factor, item_tangent, time_factor, time_tangent, send_list, tile_slot, tile_item, tile_count):
    tm, peers = lax.axis_size("tm"), lax.axis_size("user")
    rows, steps = item_factor.shape[0], time_factor.shape[0]
    tiles = rows * tm // IT
    blocks = user_factor.shape[0] // UB
    dims = (tm, peers, tiles, steps, rows)
    chunks = tm * steps // LANES
    near, held = placed(chunks == 1 and tiles <= 2)
    height = rows // peers + SUB
    packed = pl.pallas_call(
        functools.partial(pack_kernel, dims),
        out_shape=shape((tm, peers, height, R), BF16),
        in_specs=[VM] * 4 + [SM] * 4,
        out_specs=VM,
        scratch_shapes=[pltpu.VMEM((2, steps, R), F32)],
        name="pack",
    )(item_factor, item_tangent, time_factor, time_tangent, send_list, tile_slot, tile_item, tile_count)
    groups = R // SUB
    grams = pl.pallas_call(
        gram_kernel,
        out_shape=near((groups, 2 * SUB * blocks, 2 * R), BF16),
        in_specs=[VM] * 2,
        out_specs=VM,
        name="grams",
    )(user_factor, user_tangent)
    got = lax.all_to_all(
        packed.reshape(tm * peers, height, R), ("tm", "user"), split_axis=0, concat_axis=0, tiled=True
    )
    got, grams = lax.optimization_barrier((got, grams))
    other = lax.ppermute(got, "user", [(i, i ^ 1) for i in range(peers)])
    partial, wt, ww, gh, listed = pl.pallas_call(
        functools.partial(partial_kernel, dims),
        out_shape=(
            near((rows + steps, R), F32),
            near((chunks, 2 * R, LANES), BF16),
            near((chunks, LANES, R), BF16),
            near((tiles, 2 * R, R), F32),
            near((chunks, 8, LANES), jnp.int32),
        ),
        in_specs=[VM] * 3,
        out_specs=(VM,) * 5,
        scratch_shapes=[
            pltpu.VMEM(((tm + tiles) * SUB, 2 * SUB * blocks), BF16),
            pltpu.VMEM((tm, 2 * R, R), F32),
        ],
        name="partials",
    )(*held(got, other, grams))
    others = [lax.ppermute(partial, "user", [(i, i ^ d) for i in range(peers)]) for d in range(1, peers)]
    user_hvp = pl.pallas_call(
        functools.partial(user_kernel, dims),
        out_shape=shape(user_factor.shape),
        in_specs=[HBM] * 2 + [VM] * 4,
        out_specs=HBM,
        scratch_shapes=[
            pltpu.VMEM(user_factor.shape, BF16),
            pltpu.VMEM(user_factor.shape, BF16),
            pltpu.VMEM(user_factor.shape, F32),
            pltpu.VMEM((LANES // steps, 2 * R, R), F32),
            pltpu.VMEM((blocks, R, 2 * R), F32),
            pltpu.SemaphoreType.DMA((2,)),
            pltpu.SemaphoreType.DMA((4,)),
        ],
        name="user_rows",
    )(user_factor, user_tangent, *held(wt, ww, gh, listed))
    item_hvp, time_hvp = pl.pallas_call(
        functools.partial(finish_kernel, rows),
        out_shape=(shape((rows, R)), shape((steps, R))),
        in_specs=[VM] * peers,
        out_specs=(VM, VM),
        name="finish",
    )(*held(partial), *held(*others))
    return (user_hvp, item_hvp, time_hvp)


def solution(mesh):
    return jax.shard_map(
        body,
        mesh=mesh,
        in_specs=(
            P("user", None),
            P("user", None),
            P("tm", None),
            P("tm", None),
            P("tm", None),
            P("tm", None),
            P("tm", "user", None, None),
            P("tm", "user", None),
            P("tm", "user", None),
            P("tm", "user"),
        ),
        out_specs=(P("user", None), P("tm", None), P("tm", None)),
        check_vma=False,
    )
```

```python
import functools

import jax
import jax.numpy as jnp
from jax import lax
from jax.experimental import pallas as pl
from jax.experimental.pallas import tpu as pltpu
from jax.sharding import PartitionSpec as P

R = 128
UB = 128
IT = 256
LANES = 128
SUB = 8

OBS_WEIGHT = 0.03125
LAMBDA_USER = 0.5
LAMBDA_ITEM = 0.5
LAMBDA_TIME = 1.0

F32 = jnp.float32
BF16 = jnp.bfloat16
VM = pl.BlockSpec(memory_space=pltpu.VMEM)
HBM = pl.BlockSpec(memory_space=pltpu.HBM)
SM = pl.BlockSpec(memory_space=pltpu.SMEM)


def iota(shape, dim):
    return lax.broadcasted_iota(jnp.int32, shape, dim)


def dot_tn(left, right):
    return lax.dot_general(left, right, (((0,), (0,)), ((), ())), preferred_element_type=F32)


def dot_nn(left, right):
    return lax.dot_general(left, right, (((1,), (0,)), ((), ())), preferred_element_type=F32)


def halves(values):
    high = values.astype(BF16)
    return high, (values - high.astype(F32)).astype(BF16)


def dot_split(left, right):
    both = dot_nn(left, jnp.concatenate(halves(right), axis=1))
    width = right.shape[1]
    return both[:, :width] + both[:, width:]


def pack_kernel(dims, v_ref, dv_ref, w_ref, dw_ref, send_ref, slot_ref, item_ref, count_ref, out_ref, time_ref):
    tm, peers, tiles, steps, rows = dims
    me = lax.axis_index("user")
    part = rows // peers
    start = pl.multiple_of(me * part, part)
    time_ref[0, :, :] = w_ref[...].astype(F32)
    time_ref[1, :, :] = dw_ref[...].astype(F32)
    slots = send_ref.shape[3]
    row, lane = iota((SUB, LANES), 0), iota((SUB, LANES), 1)
    sent_list = jnp.zeros((SUB, LANES), jnp.int32)
    entry = lane % (peers * slots)
    for j in range(peers):
        for s in range(slots):
            sent_list = jnp.where(entry == j * slots + s, send_ref[0, 0, j, s], sent_list)
    count = count_ref[0, 0]
    at = pl.multiple_of(me // 2 * SUB, SUB)
    for k in range(peers):
        table = jnp.full((SUB, LANES), -1, jnp.int32)
        for n in range(slot_ref.shape[2]):
            hit = (lane % slots + k * slots == slot_ref[0, 0, n]) & (n < count)
            table = jnp.where(hit, item_ref[0, 0, n], table)
        lists = jnp.where(row % 4 == 0, table, sent_list).astype(F32)
        last = jnp.where(row // 4 == me % 2, time_ref[k % 2, pl.ds(at, SUB), :], lists).astype(BF16)
        first = (dv_ref if k % 2 else v_ref)[pl.ds(start, part), :]
        out_ref[:, k, :part, :] = jnp.broadcast_to(first[None], (tm, part, R))
        out_ref[:, k, part:, :] = jnp.broadcast_to(last[None], (tm, SUB, R))


def gram_kernel(u_ref, du_ref, out_ref):
    blocks = u_ref.shape[0] // UB
    groups = R // SUB

    def pair(i, carry):
        sides = []
        for g in (2 * i, 2 * i + 1):
            at = pl.ds(pl.multiple_of(g * UB, UB), UB)
            u = u_ref[at, :]
            gram = dot_tn(jnp.concatenate([u, du_ref[at, :]], axis=1), u)
            sides.append(jnp.concatenate([gram[:R], gram[R:]], axis=1).reshape(groups, SUB, 2 * R))
        high, low = halves(jnp.concatenate(sides, axis=1))
        at = pl.multiple_of(i * 2 * SUB, 2 * SUB)
        out_ref[:, pl.ds(at, 2 * SUB), :] = high
        out_ref[:, pl.ds(at + blocks * SUB, 2 * SUB), :] = low
        return carry

    lax.fori_loop(0, blocks // 2, pair, 0, unroll=2)


def dot_nt(left, right):
    return lax.dot_general(left, right, (((1,), (1,)), ((), ())), preferred_element_type=F32)


def count_rows(left, right, keep):
    counts = dot_nt(left.astype(BF16), right.astype(BF16))
    same = iota(counts.shape, 0) % SUB == iota(counts.shape, 1) % SUB
    counts = jnp.where(same, counts, 0.0).astype(BF16)
    return jnp.concatenate([counts, counts], axis=1) if keep else counts


def time_grams(wt, w, out_ref, at, steps):
    owner = iota((LANES, R), 0) // steps
    zero = jnp.zeros((LANES, R), BF16)
    for a in range(0, LANES // steps, 2):
        right = jnp.concatenate([jnp.where(owner == a + i, w, zero) for i in range(2)], axis=1)
        both = dot_nn(wt, right)
        out_ref[at + a] = both[:, :R]
        out_ref[at + a + 1] = both[:, R:]


def partial_kernel(dims, got_ref, other_ref, gram_ref, out_ref, wt_ref, ww_ref, gh_ref, entry_ref, left_ref, grams_ref):
    tm, peers, tiles, steps, rows = dims
    groups, depth = gram_ref.shape[:2]
    blocks = depth // (2 * SUB)
    part = rows // peers
    entries = LANES // steps
    chunks = tm // entries
    me_tm, me = lax.axis_index("tm"), lax.axis_index("user")
    lane, row8 = iota((8, LANES), 1), iota((8, LANES), 0)
    slots = steps // peers
    even = me % 2 == 0
    group = lane // slots % peers

    def sent(a, j, kind):
        here = a * peers + j
        return jnp.where(even == (kind == 0), got_ref[here, :part, :], other_ref[here, :part, :])

    def time_rows_of(a):
        lasts = [[ref[a * peers + j, part:, :].astype(F32) for j in range(peers)] for ref in (got_ref, other_ref)]
        sides = []
        for kind in range(2):
            pieces = [jnp.where(even == (kind == 0), lasts[0][j], lasts[1][j]) for j in range(peers)]
            sides.append(jnp.concatenate([jnp.where(row8 < 4, *pieces[j : j + 2]) for j in range(0, peers, 2)], axis=0))
        return sides, lasts[0]

    my_tile = me_tm * rows // IT

    coeff_rows = me_tm * steps + iota((steps, LANES), 0)
    penalty = jnp.zeros((steps, R), F32)
    total_steps = tm * steps
    item_height = entries * SUB
    own_counts = jnp.zeros((tiles * SUB, blocks * SUB), BF16)
    for chunk in range(chunks):
        base = chunk * entries
        found_m = jnp.zeros((8, LANES), F32)
        found_g = jnp.zeros((8, LANES), F32)
        sides = ([], [])
        for a in range(entries):
            both, lasts = time_rows_of(base + a)
            sides[0].append(both[0])
            sides[1].append(both[1])
            mine = lane // steps == a
            tile = lasts[0]
            for j in range(1, peers):
                tile = jnp.where(group == j, lasts[j], tile)
            found_m = jnp.where(mine, tile, found_m)
            own_list = got_ref[(base + a) * peers + me, part:, :].astype(F32)
            found_g = jnp.where(mine, own_list, found_g)
        found_m = jnp.where(row8 == jnp.where(group % 2 == 0, 4, 0), found_m, 0.0)
        found_g = jnp.where(row8 == jnp.where(even, 5, 1), found_g, 0.0)
        w, dw = jnp.concatenate(sides[0], axis=0), jnp.concatenate(sides[1], axis=0)
        wt_ref[chunk] = jnp.concatenate([w, dw], axis=1).T.astype(BF16)
        ww_ref[chunk] = w.astype(BF16)
        time_grams(wt_ref[chunk], ww_ref[chunk], grams_ref, base, steps)
        item = jnp.sum(found_m, axis=0, keepdims=True).astype(jnp.int32)
        block = jnp.sum(found_g, axis=0, keepdims=True).astype(jnp.int32)
        entry_ref[chunk, 0:1, :] = item
        entry_ref[chunk, 1:2, :] = block
        shape_left, shape_right = (item_height, LANES), (blocks * SUB, LANES)
        right = block == iota(shape_right, 0) // SUB
        left = (iota(shape_left, 1) // steps == iota(shape_left, 0) // SUB) & (item == my_tile)
        left_ref[pl.ds(chunk * item_height, item_height), :] = count_rows(left, right, True)
        shape_left = (tiles * SUB, LANES)
        left = (iota(shape_left, 1) // steps == me_tm - base) & (item == iota(shape_left, 0) // SUB)
        own_counts = own_counts + count_rows(left, right, False)
        column = chunk * LANES + iota((steps, LANES), 1)
        coeff = jnp.zeros((steps, LANES), F32)
        for shift, scale in ((-1, 1.0), (0, -2.0), (1, 1.0)):
            centre = coeff_rows + shift
            inside = (centre >= 1) & (centre <= total_steps - 2)
            apart = column - centre
            value = jnp.where(apart == 0, -2.0, jnp.where(jnp.abs(apart) == 1, 1.0, 0.0))
            coeff = coeff + jnp.where(inside, scale * value, 0.0)
        penalty = penalty + dot_nn(coeff.astype(BF16), dw.astype(BF16))
    left_ref[pl.ds(chunks * item_height, tiles * SUB), :] = jnp.concatenate([own_counts, own_counts], axis=1)

    per_tile = IT // rows

    def item_grams(m, carry):
        def gathered(kind):
            return jnp.concatenate([sent(m * per_tile + a, j, kind) for a in range(per_tile) for j in range(peers)], axis=0)

        v = gathered(0)
        gh_ref[m] = OBS_WEIGHT * dot_tn(jnp.concatenate([v, gathered(1)], axis=1), v)
        return carry

    lax.fori_loop(0, tiles, item_grams, 0, unroll=tiles <= 2)

    sides = ([], [], [], [])
    for group in range(groups):
        sums = dot_nn(left_ref[...], gram_ref[group])
        s, d = sums[:, :R], sums[:, R:]
        at = pl.ds(group * SUB, SUB)
        below = pl.ds(R + group * SUB, SUB)
        a_rows = b_rows = q_rows = r_rows = jnp.zeros((SUB, R), F32)
        for a in range(tm):
            here = slice(a * SUB, (a + 1) * SUB)
            y, z = grams_ref[a, at, :], grams_ref[a, below, :]
            a_rows = a_rows + d[here] * y + s[here] * z
            b_rows = b_rows + s[here] * y
        for m in range(tiles):
            here = slice((tm + m) * SUB, (tm + m + 1) * SUB)
            g_m, h_m = gh_ref[m, at, :], gh_ref[m, below, :]
            q_rows = q_rows + d[here] * g_m + s[here] * h_m
            r_rows = r_rows + s[here] * g_m
        for side, value in zip(sides, (a_rows, b_rows, q_rows, r_rows)):
            side.append(value)
    v_own = jnp.concatenate([sent(me_tm, j, 0) for j in range(peers)], axis=0)
    dv_own = jnp.concatenate([sent(me_tm, j, 1) for j in range(peers)], axis=0)
    left = jnp.concatenate([v_own, dv_own], axis=1)
    item_rows = OBS_WEIGHT * dot_split(left, jnp.concatenate(sides[0] + sides[1], axis=0))
    left = jnp.concatenate(time_rows_of(me_tm)[0], axis=1)
    time_rows = dot_split(left.astype(BF16), jnp.concatenate(sides[2] + sides[3], axis=0))
    first = jnp.where(me == 0, 1.0, 0.0)
    out_ref[:rows, :] = item_rows + (first * LAMBDA_ITEM) * dv_own.astype(F32)
    out_ref[rows:, :] = time_rows + (first * LAMBDA_TIME) * penalty


def user_kernel(dims, u_hbm, du_hbm, wt_ref, ww_ref, gh_ref, entry_ref, out_hbm, u_ref, du_ref, out_ref, grams_ref, k_ref, in_sem, out_sem):
    tm, peers, tiles, steps, rows = dims
    chunks = wt_ref.shape[0]
    entries = LANES // steps
    blocks, groups = k_ref.shape[0], R // SUB
    loads = [
        pltpu.make_async_copy(u_hbm, u_ref, in_sem.at[0]),
        pltpu.make_async_copy(du_hbm, du_ref, in_sem.at[1]),
    ]
    for load in loads:
        load.start()

    width = LANES // (entries * SUB)

    def add(chunk, first, fresh):
        item, block = entry_ref[chunk, 0:1, :], entry_ref[chunk, 1:2, :]
        left = block == iota((blocks * SUB, LANES), 0) // SUB
        shape_right = (entries * width * SUB, LANES)
        place = iota(shape_right, 0) // SUB
        right = (iota(shape_right, 1) // steps == place // width) & (item == first + place % width)
        counts = count_rows(left, right, True)
        def rows_of(group, carry):
            at = pl.ds(pl.multiple_of(group * SUB, SUB), SUB)
            below = pl.ds(pl.multiple_of(R + group * SUB, SUB), SUB)
            stack = []
            for a in range(entries):
                y, z = grams_ref[a, at, :], grams_ref[a, below, :]
                for m in range(width):
                    g_m, h_m = gh_ref[first + m, at, :], gh_ref[first + m, below, :]
                    stack.append(jnp.concatenate([g_m * y, g_m * z + h_m * y], axis=1))
            high, low = halves(jnp.concatenate(stack, axis=0))
            value = dot_nn(counts, jnp.concatenate([high, low], axis=0)).reshape(blocks, SUB, 2 * R)
            if fresh:
                eye = iota((SUB, 2 * R), 0) + group * SUB == iota((SUB, 2 * R), 1)
                value = value + jnp.where(eye, LAMBDA_USER, 0.0)[None]
            k_ref[:, at, :] = value if fresh else k_ref[:, at, :] + value
            return carry

        lax.fori_loop(0, groups, rows_of, 0, unroll=8)

    for chunk in range(chunks):
        time_grams(wt_ref[chunk], ww_ref[chunk], grams_ref, 0, steps)
        add(chunk, 0, chunk == 0)

        def rest(i, carry):
            add(chunk, i * width, False)
            return carry

        lax.fori_loop(1, tiles // width, rest, 0)

    for load in loads:
        load.wait()
    stores = []
    per_store = blocks // out_sem.shape[0]
    for number in range(out_sem.shape[0]):
        for g in range(number * per_store, (number + 1) * per_store):
            at = pl.ds(g * UB, UB)
            left = jnp.concatenate([du_ref[at, :], u_ref[at, :]], axis=1)
            out_ref[at, :] = dot_split(left, jnp.concatenate([k_ref[g, :, :R], k_ref[g, :, R:]], axis=0))
        at = pl.ds(number * per_store * UB, per_store * UB)
        store = pltpu.make_async_copy(out_ref.at[at, :], out_hbm.at[at, :], out_sem.at[number])
        store.start()
        stores.append(store)
    for store in stores:
        store.wait()


def finish_kernel(rows, *refs):
    item_ref, time_ref = refs[-2:]
    item_ref[...] = functools.reduce(jnp.add, [ref[:rows, :] for ref in refs[:-2]])
    time_ref[...] = functools.reduce(jnp.add, [ref[rows:, :] for ref in refs[:-2]])


def shape(dims, dtype=F32):
    return jax.ShapeDtypeStruct(dims, dtype)


def placed(small):
    if not small:
        return shape, lambda *arrays: arrays
    return pltpu.VMEM, lambda *arrays: [pltpu.with_memory_space_constraint(x, pltpu.VMEM) for x in arrays]


def body(user_factor, user_tangent, item_factor, item_tangent, time_factor, time_tangent, send_list, tile_slot, tile_item, tile_count):
    tm, peers = lax.axis_size("tm"), lax.axis_size("user")
    rows, steps = item_factor.shape[0], time_factor.shape[0]
    tiles = rows * tm // IT
    blocks = user_factor.shape[0] // UB
    dims = (tm, peers, tiles, steps, rows)
    chunks = tm * steps // LANES
    near, held = placed(chunks == 1 and tiles <= 2)
    height = rows // peers + SUB
    packed = pl.pallas_call(
        functools.partial(pack_kernel, dims),
        out_shape=shape((tm, peers, height, R), BF16),
        in_specs=[VM] * 4 + [SM] * 4,
        out_specs=VM,
        scratch_shapes=[pltpu.VMEM((2, steps, R), F32)],
        name="pack",
    )(item_factor, item_tangent, time_factor, time_tangent, send_list, tile_slot, tile_item, tile_count)
    groups = R // SUB
    grams = pl.pallas_call(
        gram_kernel,
        out_shape=near((groups, 2 * SUB * blocks, 2 * R), BF16),
        in_specs=[VM] * 2,
        out_specs=VM,
        name="grams",
    )(user_factor, user_tangent)
    got = lax.all_to_all(
        packed.reshape(tm * peers, height, R), ("tm", "user"), split_axis=0, concat_axis=0, tiled=True
    )
    got, grams = lax.optimization_barrier((got, grams))
    other = lax.ppermute(got, "user", [(i, i ^ 1) for i in range(peers)])
    partial, wt, ww, gh, listed = pl.pallas_call(
        functools.partial(partial_kernel, dims),
        out_shape=(
            near((rows + steps, R), F32),
            near((chunks, 2 * R, LANES), BF16),
            near((chunks, LANES, R), BF16),
            near((tiles, 2 * R, R), F32),
            near((chunks, 8, LANES), jnp.int32),
        ),
        in_specs=[VM] * 3,
        out_specs=(VM,) * 5,
        scratch_shapes=[
            pltpu.VMEM(((tm + tiles) * SUB, 2 * SUB * blocks), BF16),
            pltpu.VMEM((tm, 2 * R, R), F32),
        ],
        name="partials",
    )(*held(got, other, grams))
    others = [lax.ppermute(partial, "user", [(i, i ^ d) for i in range(peers)]) for d in range(1, peers)]
    user_hvp = pl.pallas_call(
        functools.partial(user_kernel, dims),
        out_shape=shape(user_factor.shape),
        in_specs=[HBM] * 2 + [VM] * 4,
        out_specs=HBM,
        scratch_shapes=[
            pltpu.VMEM(user_factor.shape, BF16),
            pltpu.VMEM(user_factor.shape, BF16),
            pltpu.VMEM(user_factor.shape, F32),
            pltpu.VMEM((LANES // steps, 2 * R, R), F32),
            pltpu.VMEM((blocks, R, 2 * R), F32),
            pltpu.SemaphoreType.DMA((2,)),
            pltpu.SemaphoreType.DMA((4,)),
        ],
        name="user_rows",
    )(user_factor, user_tangent, *held(wt, ww, gh, listed))
    item_hvp, time_hvp = pl.pallas_call(
        functools.partial(finish_kernel, rows),
        out_shape=(shape((rows, R)), shape((steps, R))),
        in_specs=[VM] * peers,
        out_specs=(VM, VM),
        name="finish",
    )(*held(partial), *held(*others))
    return (user_hvp, item_hvp, time_hvp)


def solution(mesh):
    return jax.shard_map(
        body,
        mesh=mesh,
        in_specs=(
            P("user", None),
            P("user", None),
            P("tm", None),
            P("tm", None),
            P("tm", None),
            P("tm", None),
            P("tm", "user", None, None),
            P("tm", "user", None),
            P("tm", "user", None),
            P("tm", "user"),
        ),
        out_specs=(P("user", None), P("tm", None), P("tm", None)),
        check_vma=False,
    )
```

```python
import functools

import jax
import jax.numpy as jnp
from jax import lax
from jax.experimental import pallas as pl
from jax.experimental.pallas import tpu as pltpu
from jax.sharding import PartitionSpec as P

R = 128
UB = 128
IT = 256
LANES = 128
SUB = 8

OBS_WEIGHT = 0.03125
LAMBDA_USER = 0.5
LAMBDA_ITEM = 0.5
LAMBDA_TIME = 1.0

F32 = jnp.float32
BF16 = jnp.bfloat16
VM = pl.BlockSpec(memory_space=pltpu.VMEM)
HBM = pl.BlockSpec(memory_space=pltpu.HBM)
SM = pl.BlockSpec(memory_space=pltpu.SMEM)


def iota(shape, dim):
    return lax.broadcasted_iota(jnp.int32, shape, dim)


def dot_tn(left, right):
    return lax.dot_general(left, right, (((0,), (0,)), ((), ())), preferred_element_type=F32)


def dot_nn(left, right):
    return lax.dot_general(left, right, (((1,), (0,)), ((), ())), preferred_element_type=F32)


def halves(values):
    high = values.astype(BF16)
    return high, (values - high.astype(F32)).astype(BF16)


def dot_split(left, right):
    both = dot_nn(left, jnp.concatenate(halves(right), axis=1))
    width = right.shape[1]
    return both[:, :width] + both[:, width:]


def pack_kernel(dims, v_ref, dv_ref, w_ref, dw_ref, send_ref, slot_ref, item_ref, count_ref, out_ref, time_ref):
    tm, peers, tiles, steps, rows = dims
    me = lax.axis_index("user")
    part = rows // peers
    start = pl.multiple_of(me * part, part)
    time_ref[0, :, :] = w_ref[...].astype(F32)
    time_ref[1, :, :] = dw_ref[...].astype(F32)
    slots = send_ref.shape[3]
    row, lane = iota((SUB, LANES), 0), iota((SUB, LANES), 1)
    sent_list = jnp.zeros((SUB, LANES), jnp.int32)
    entry = lane % (peers * slots)
    for j in range(peers):
        for s in range(slots):
            sent_list = jnp.where(entry == j * slots + s, send_ref[0, 0, j, s], sent_list)
    count = count_ref[0, 0]
    at = pl.multiple_of(me // 2 * SUB, SUB)
    for k in range(peers):
        table = jnp.full((SUB, LANES), -1, jnp.int32)
        for n in range(slot_ref.shape[2]):
            hit = (lane % slots + k * slots == slot_ref[0, 0, n]) & (n < count)
            table = jnp.where(hit, item_ref[0, 0, n], table)
        lists = jnp.where(row % 4 == 0, table, sent_list).astype(F32)
        last = jnp.where(row // 4 == me % 2, time_ref[k % 2, pl.ds(at, SUB), :], lists).astype(BF16)
        first = (dv_ref if k % 2 else v_ref)[pl.ds(start, part), :]
        out_ref[:, k, :part, :] = jnp.broadcast_to(first[None], (tm, part, R))
        out_ref[:, k, part:, :] = jnp.broadcast_to(last[None], (tm, SUB, R))


def gram_kernel(u_ref, du_ref, out_ref):
    blocks = u_ref.shape[0] // UB
    groups = R // SUB

    def pair(i, carry):
        sides = []
        for g in (2 * i, 2 * i + 1):
            at = pl.ds(pl.multiple_of(g * UB, UB), UB)
            u = u_ref[at, :]
            gram = dot_tn(jnp.concatenate([u, du_ref[at, :]], axis=1), u)
            sides.append(jnp.concatenate([gram[:R], gram[R:]], axis=1).reshape(groups, SUB, 2 * R))
        high, low = halves(jnp.concatenate(sides, axis=1))
        at = pl.multiple_of(i * 2 * SUB, 2 * SUB)
        out_ref[:, pl.ds(at, 2 * SUB), :] = high
        out_ref[:, pl.ds(at + blocks * SUB, 2 * SUB), :] = low
        return carry

    lax.fori_loop(0, blocks // 2, pair, 0, unroll=2)


def dot_nt(left, right):
    return lax.dot_general(left, right, (((1,), (1,)), ((), ())), preferred_element_type=F32)


def count_rows(left, right, keep):
    counts = dot_nt(left.astype(BF16), right.astype(BF16))
    same = iota(counts.shape, 0) % SUB == iota(counts.shape, 1) % SUB
    counts = jnp.where(same, counts, 0.0).astype(BF16)
    return jnp.concatenate([counts, counts], axis=1) if keep else counts


def time_grams(wt, w, out_ref, at, steps):
    owner = iota((LANES, R), 0) // steps
    zero = jnp.zeros((LANES, R), BF16)
    for a in range(0, LANES // steps, 2):
        right = jnp.concatenate([jnp.where(owner == a + i, w, zero) for i in range(2)], axis=1)
        both = dot_nn(wt, right)
        out_ref[at + a] = both[:, :R]
        out_ref[at + a + 1] = both[:, R:]


def partial_kernel(dims, got_ref, other_ref, gram_ref, out_ref, wt_ref, ww_ref, gh_ref, entry_ref, left_ref, grams_ref):
    tm, peers, tiles, steps, rows = dims
    groups, depth = gram_ref.shape[:2]
    blocks = depth // (2 * SUB)
    part = rows // peers
    entries = LANES // steps
    chunks = tm // entries
    me_tm, me = lax.axis_index("tm"), lax.axis_index("user")
    lane, row8 = iota((8, LANES), 1), iota((8, LANES), 0)
    slots = steps // peers
    even = me % 2 == 0
    group = lane // slots % peers

    def sent(a, j, kind):
        here = a * peers + j
        return jnp.where(even == (kind == 0), got_ref[here, :part, :], other_ref[here, :part, :])

    def time_rows_of(a):
        lasts = [[ref[a * peers + j, part:, :].astype(F32) for j in range(peers)] for ref in (got_ref, other_ref)]
        sides = []
        for kind in range(2):
            pieces = [jnp.where(even == (kind == 0), lasts[0][j], lasts[1][j]) for j in range(peers)]
            sides.append(jnp.concatenate([jnp.where(row8 < 4, *pieces[j : j + 2]) for j in range(0, peers, 2)], axis=0))
        return sides, lasts[0]

    my_tile = me_tm * rows // IT

    coeff_rows = me_tm * steps + iota((steps, LANES), 0)
    penalty = jnp.zeros((steps, R), F32)
    total_steps = tm * steps
    item_height = entries * SUB
    own_counts = jnp.zeros((tiles * SUB, blocks * SUB), BF16)
    for chunk in range(chunks):
        base = chunk * entries
        found_m = jnp.zeros((8, LANES), F32)
        found_g = jnp.zeros((8, LANES), F32)
        sides = ([], [])
        for a in range(entries):
            both, lasts = time_rows_of(base + a)
            sides[0].append(both[0])
            sides[1].append(both[1])
            mine = lane // steps == a
            tile = lasts[0]
            for j in range(1, peers):
                tile = jnp.where(group == j, lasts[j], tile)
            found_m = jnp.where(mine, tile, found_m)
            own_list = got_ref[(base + a) * peers + me, part:, :].astype(F32)
            found_g = jnp.where(mine, own_list, found_g)
        found_m = jnp.where(row8 == jnp.where(group % 2 == 0, 4, 0), found_m, 0.0)
        found_g = jnp.where(row8 == jnp.where(even, 5, 1), found_g, 0.0)
        w, dw = jnp.concatenate(sides[0], axis=0), jnp.concatenate(sides[1], axis=0)
        wt_ref[chunk] = jnp.concatenate([w, dw], axis=1).T.astype(BF16)
        ww_ref[chunk] = w.astype(BF16)
        time_grams(wt_ref[chunk], ww_ref[chunk], grams_ref, base, steps)
        item = jnp.sum(found_m, axis=0, keepdims=True).astype(jnp.int32)
        block = jnp.sum(found_g, axis=0, keepdims=True).astype(jnp.int32)
        entry_ref[chunk, 0:1, :] = item
        entry_ref[chunk, 1:2, :] = block
        shape_left, shape_right = (item_height, LANES), (blocks * SUB, LANES)
        right = block == iota(shape_right, 0) // SUB
        left = (iota(shape_left, 1) // steps == iota(shape_left, 0) // SUB) & (item == my_tile)
        left_ref[pl.ds(chunk * item_height, item_height), :] = count_rows(left, right, True)
        shape_left = (tiles * SUB, LANES)
        left = (iota(shape_left, 1) // steps == me_tm - base) & (item == iota(shape_left, 0) // SUB)
        own_counts = own_counts + count_rows(left, right, False)
        column = chunk * LANES + iota((steps, LANES), 1)
        coeff = jnp.zeros((steps, LANES), F32)
        for shift, scale in ((-1, 1.0), (0, -2.0), (1, 1.0)):
            centre = coeff_rows + shift
            inside = (centre >= 1) & (centre <= total_steps - 2)
            apart = column - centre
            value = jnp.where(apart == 0, -2.0, jnp.where(jnp.abs(apart) == 1, 1.0, 0.0))
            coeff = coeff + jnp.where(inside, scale * value, 0.0)
        penalty = penalty + dot_nn(coeff.astype(BF16), dw.astype(BF16))
    left_ref[pl.ds(chunks * item_height, tiles * SUB), :] = jnp.concatenate([own_counts, own_counts], axis=1)

    per_tile = IT // rows

    def item_grams(m, carry):
        def gathered(kind):
            return jnp.concatenate([sent(m * per_tile + a, j, kind) for a in range(per_tile) for j in range(peers)], axis=0)

        v = gathered(0)
        gh_ref[m] = OBS_WEIGHT * dot_tn(jnp.concatenate([v, gathered(1)], axis=1), v)
        return carry

    lax.fori_loop(0, tiles, item_grams, 0, unroll=tiles <= 2)

    sides = ([], [], [], [])
    for group in range(groups):
        sums = dot_nn(left_ref[...], gram_ref[group])
        s, d = sums[:, :R], sums[:, R:]
        at = pl.ds(group * SUB, SUB)
        below = pl.ds(R + group * SUB, SUB)
        a_rows = b_rows = q_rows = r_rows = jnp.zeros((SUB, R), F32)
        for a in range(tm):
            here = slice(a * SUB, (a + 1) * SUB)
            y, z = grams_ref[a, at, :], grams_ref[a, below, :]
            a_rows = a_rows + d[here] * y + s[here] * z
            b_rows = b_rows + s[here] * y
        for m in range(tiles):
            here = slice((tm + m) * SUB, (tm + m + 1) * SUB)
            g_m, h_m = gh_ref[m, at, :], gh_ref[m, below, :]
            q_rows = q_rows + d[here] * g_m + s[here] * h_m
            r_rows = r_rows + s[here] * g_m
        for side, value in zip(sides, (a_rows, b_rows, q_rows, r_rows)):
            side.append(value)
    v_own = jnp.concatenate([sent(me_tm, j, 0) for j in range(peers)], axis=0)
    dv_own = jnp.concatenate([sent(me_tm, j, 1) for j in range(peers)], axis=0)
    left = jnp.concatenate([v_own, dv_own], axis=1)
    item_rows = OBS_WEIGHT * dot_split(left, jnp.concatenate(sides[0] + sides[1], axis=0))
    left = jnp.concatenate(time_rows_of(me_tm)[0], axis=1)
    time_rows = dot_split(left.astype(BF16), jnp.concatenate(sides[2] + sides[3], axis=0))
    first = jnp.where(me == 0, 1.0, 0.0)
    out_ref[:rows, :] = item_rows + (first * LAMBDA_ITEM) * dv_own.astype(F32)
    out_ref[rows:, :] = time_rows + (first * LAMBDA_TIME) * penalty


def user_kernel(dims, u_hbm, du_hbm, wt_ref, ww_ref, gh_ref, entry_ref, out_hbm, u_ref, du_ref, out_ref, grams_ref, k_ref, in_sem, out_sem):
    tm, peers, tiles, steps, rows = dims
    chunks = wt_ref.shape[0]
    entries = LANES // steps
    blocks, groups = k_ref.shape[0], R // SUB
    loads = [
        pltpu.make_async_copy(u_hbm, u_ref, in_sem.at[0]),
        pltpu.make_async_copy(du_hbm, du_ref, in_sem.at[1]),
    ]
    for load in loads:
        load.start()

    width = LANES // (entries * SUB)

    def add(chunk, first, fresh):
        item, block = entry_ref[chunk, 0:1, :], entry_ref[chunk, 1:2, :]
        left = block == iota((blocks * SUB, LANES), 0) // SUB
        shape_right = (entries * width * SUB, LANES)
        place = iota(shape_right, 0) // SUB
        right = (iota(shape_right, 1) // steps == place // width) & (item == first + place % width)
        counts = count_rows(left, right, True)
        def rows_of(group, carry):
            at = pl.ds(pl.multiple_of(group * SUB, SUB), SUB)
            below = pl.ds(pl.multiple_of(R + group * SUB, SUB), SUB)
            stack = []
            for a in range(entries):
                y, z = grams_ref[a, at, :], grams_ref[a, below, :]
                for m in range(width):
                    g_m, h_m = gh_ref[first + m, at, :], gh_ref[first + m, below, :]
                    stack.append(jnp.concatenate([g_m * y, g_m * z + h_m * y], axis=1))
            high, low = halves(jnp.concatenate(stack, axis=0))
            value = dot_nn(counts, jnp.concatenate([high, low], axis=0)).reshape(blocks, SUB, 2 * R)
            if fresh:
                eye = iota((SUB, 2 * R), 0) + group * SUB == iota((SUB, 2 * R), 1)
                value = value + jnp.where(eye, LAMBDA_USER, 0.0)[None]
            k_ref[:, at, :] = value if fresh else k_ref[:, at, :] + value
            return carry

        lax.fori_loop(0, groups, rows_of, 0, unroll=8)

    for chunk in range(chunks):
        time_grams(wt_ref[chunk], ww_ref[chunk], grams_ref, 0, steps)
        add(chunk, 0, chunk == 0)

        def rest(i, carry):
            add(chunk, i * width, False)
            return carry

        lax.fori_loop(1, tiles // width, rest, 0)

    for load in loads:
        load.wait()
    stores = []
    per_store = blocks // out_sem.shape[0]
    for number in range(out_sem.shape[0]):
        for g in range(number * per_store, (number + 1) * per_store):
            at = pl.ds(g * UB, UB)
            left = jnp.concatenate([du_ref[at, :], u_ref[at, :]], axis=1)
            out_ref[at, :] = dot_split(left, jnp.concatenate([k_ref[g, :, :R], k_ref[g, :, R:]], axis=0))
        at = pl.ds(number * per_store * UB, per_store * UB)
        store = pltpu.make_async_copy(out_ref.at[at, :], out_hbm.at[at, :], out_sem.at[number])
        store.start()
        stores.append(store)
    for store in stores:
        store.wait()


def finish_kernel(rows, *refs):
    item_ref, time_ref = refs[-2:]
    item_ref[...] = functools.reduce(jnp.add, [ref[:rows, :] for ref in refs[:-2]])
    time_ref[...] = functools.reduce(jnp.add, [ref[rows:, :] for ref in refs[:-2]])


def shape(dims, dtype=F32):
    return jax.ShapeDtypeStruct(dims, dtype)


def placed(small):
    if not small:
        return shape, lambda *arrays: arrays
    return pltpu.VMEM, lambda *arrays: [pltpu.with_memory_space_constraint(x, pltpu.VMEM) for x in arrays]


def body(user_factor, user_tangent, item_factor, item_tangent, time_factor, time_tangent, send_list, tile_slot, tile_item, tile_count):
    tm, peers = lax.axis_size("tm"), lax.axis_size("user")
    rows, steps = item_factor.shape[0], time_factor.shape[0]
    tiles = rows * tm // IT
    blocks = user_factor.shape[0] // UB
    dims = (tm, peers, tiles, steps, rows)
    chunks = tm * steps // LANES
    near, held = placed(chunks == 1 and tiles <= 2)
    height = rows // peers + SUB
    packed = pl.pallas_call(
        functools.partial(pack_kernel, dims),
        out_shape=shape((tm, peers, height, R), BF16),
        in_specs=[VM] * 4 + [SM] * 4,
        out_specs=VM,
        scratch_shapes=[pltpu.VMEM((2, steps, R), F32)],
        name="pack",
    )(item_factor, item_tangent, time_factor, time_tangent, send_list, tile_slot, tile_item, tile_count)
    groups = R // SUB
    grams = pl.pallas_call(
        gram_kernel,
        out_shape=near((groups, 2 * SUB * blocks, 2 * R), BF16),
        in_specs=[VM] * 2,
        out_specs=VM,
        name="grams",
    )(user_factor, user_tangent)
    got = lax.all_to_all(
        packed.reshape(tm * peers, height, R), ("tm", "user"), split_axis=0, concat_axis=0, tiled=True
    )
    got, grams = lax.optimization_barrier((got, grams))
    other = lax.ppermute(got, "user", [(i, i ^ 1) for i in range(peers)])
    partial, wt, ww, gh, listed = pl.pallas_call(
        functools.partial(partial_kernel, dims),
        out_shape=(
            near((rows + steps, R), F32),
            near((chunks, 2 * R, LANES), BF16),
            near((chunks, LANES, R), BF16),
            near((tiles, 2 * R, R), F32),
            near((chunks, 8, LANES), jnp.int32),
        ),
        in_specs=[VM] * 3,
        out_specs=(VM,) * 5,
        scratch_shapes=[
            pltpu.VMEM(((tm + tiles) * SUB, 2 * SUB * blocks), BF16),
            pltpu.VMEM((tm, 2 * R, R), F32),
        ],
        name="partials",
    )(*held(got, other, grams))
    others = [lax.ppermute(partial, "user", [(i, i ^ d) for i in range(peers)]) for d in range(1, peers)]
    user_hvp = pl.pallas_call(
        functools.partial(user_kernel, dims),
        out_shape=shape(user_factor.shape),
        in_specs=[HBM] * 2 + [VM] * 4,
        out_specs=HBM,
        scratch_shapes=[
            pltpu.VMEM(user_factor.shape, BF16),
            pltpu.VMEM(user_factor.shape, BF16),
            pltpu.VMEM(user_factor.shape, F32),
            pltpu.VMEM((LANES // steps, 2 * R, R), F32),
            pltpu.VMEM((blocks, R, 2 * R), F32),
            pltpu.SemaphoreType.DMA((2,)),
            pltpu.SemaphoreType.DMA((8,)),
        ],
        name="user_rows",
    )(user_factor, user_tangent, *held(wt, ww, gh, listed))
    item_hvp, time_hvp = pl.pallas_call(
        functools.partial(finish_kernel, rows),
        out_shape=(shape((rows, R)), shape((steps, R))),
        in_specs=[VM] * peers,
        out_specs=(VM, VM),
        name="finish",
    )(*held(partial), *held(*others))
    return (user_hvp, item_hvp, time_hvp)


def solution(mesh):
    return jax.shard_map(
        body,
        mesh=mesh,
        in_specs=(
            P("user", None),
            P("user", None),
            P("tm", None),
            P("tm", None),
            P("tm", None),
            P("tm", None),
            P("tm", "user", None, None),
            P("tm", "user", None),
            P("tm", "user", None),
            P("tm", "user"),
        ),
        out_specs=(P("user", None), P("tm", None), P("tm", None)),
        check_vma=False,
    )
```
